32 devices in a mesh: segment: 4 (over y, x), seq: 8 (over z, core).
Axes of the slice: x: 2, y: 2, z: 4, core: 2. Of those that a mesh axis runs over, the one named last changes fastest.
Arguments:
- hidden: bfloat16 [4, 8192, 8192], P('segment', 'seq'), may hold values from -6 to 6
- span_lengths: int32 [4, 64], replicated, may hold values from 1 to 512, 8192 in all within a row
- section_of: int32 [4, 64], replicated, may hold values from 0 to 31
- section_live: int32 [32], P('seq'), may hold values 0 or 1
- w_in: bfloat16 [8192, 2048], P('seq'), may hold values from -0.5 to 0.5
- norm_gain: float32 [2048], replicated, may hold values from 0.5 to 1.5
- w_query: bfloat16 [2048, 2048], P(None, 'segment'), may hold values from -0.125 to 0.125
- w_key: bfloat16 [2048, 2048], P(None, 'segment'), may hold values from -0.125 to 0.125
- w_value: bfloat16 [2048, 2048], P(None, 'segment'), may hold values from -0.125 to 0.125
- w_out: bfloat16 [2048, 2048], P('segment'), may hold values from -0.125 to 0.125
Outputs:
- section_out: bfloat16 [32, 2048], P('seq')
The draws below stay inside these ranges and needn't reach their ends.
All inputs are finite; a program needn't handle non-finite values. No bound on the sum of `section_live` on one device may be relied on, other than what follows from the above.
Results may differ from the reference program's by a relative error of at most 0.007.
Values may be sent and summed in bfloat16 or wider, within the bound.
A program may use at most 128 MiB of HBM per device.

```python
import math
import jax
import jax.numpy as jnp
import numpy as np
from jax import lax

D = 8192
DS = 2048
HEADS = 16
HEAD_DIM = 128
SPAN_MAX = 512
DOCS = 4
L = 8192
NCH = 64
NSEC = 32


def with_ends(entries, own_key, smallest, largest):
    longest = entries.shape.index(max(entries.shape))
    spots = []
    for shift in (0, 1):
        where = [jax.random.randint(jax.random.fold_in(own_key, axis), (), 0, length) for axis, length in enumerate(entries.shape)]
        where[longest] = (where[longest] + shift) % entries.shape[longest]
        spots.append(tuple(where))
    return entries.at[spots[0]].set(smallest).at[spots[1]].set(largest)


def levels(rng, extent, pieces, low, top_value):
    gain = 1.0
    for position, blocks in pieces:
        steps = jax.random.uniform(jax.random.fold_in(jax.random.fold_in(rng, 6), position), (blocks,), jnp.float32, low / len(pieces), top_value / len(pieces))
        gain = gain * jnp.repeat(jnp.exp(steps), extent[position] // blocks).reshape((-1,) + (1,) * (len(extent) - 1 - position))
    return gain


def rank_table(amount, slope):
    weights = [(1 << 20) // math.isqrt(rank ** slope) + 1 for rank in range(1, amount + 1)]
    spread = 1 + sum(weights) // (1 << 30)
    return np.cumsum(np.array([max(1, weight // spread) for weight in weights]))


def skewed_ids(stream_key, shape, amount, skew):
    grid = rank_table(amount, skew)
    ticket = jax.random.randint(jax.random.fold_in(stream_key, 1), shape, 0, int(grid[amount - 1]))
    rank = jnp.searchsorted(jnp.asarray(grid, jnp.int32), ticket, side="right")
    return jax.random.permutation(jax.random.fold_in(stream_key, 2), amount)[rank].astype(jnp.int32)


def profile(count, total, most, slope):
    weights = [(1 << 20) // math.isqrt(standing ** slope) + 1 for standing in range(2, count + 1)]
    surplus, given = total - most - (count - 1), [1] * (count - 1)
    while surplus > 0:
        free = [i for i in range(count - 1) if given[i] < most]
        pool, remaining = sum([weights[i] for i in free]), surplus
        for i in free:
            extra = min(most - given[i], max(1, remaining * weights[i] // pool), surplus)
            given[i] = given[i] + extra
            surplus = surplus - extra
    return np.array([most] + given)


def ragged_sizes(rng, number_of, total, most, lean):
    if number_of == 2:
        one = jax.random.randint(rng, (), max(1, total - most), min(most, total - 1) + 1)
        return jnp.stack([one, total - one])
    lengths = jnp.asarray(profile(number_of, total, most, lean), jnp.int32)
    pairs = (number_of - 1) // 2
    donor, receiver = lengths[1:1 + 2 * pairs:2], lengths[2:2 + 2 * pairs:2]
    room = jnp.minimum(donor - 1, most - receiver)
    passed = jax.random.randint(jax.random.fold_in(rng, 1), (pairs,), 0, 1 << 20) % (room + 1)
    lengths = lengths.at[1:1 + 2 * pairs:2].set(donor - passed).at[2:2 + 2 * pairs:2].set(receiver + passed)
    return lengths[jax.random.permutation(jax.random.fold_in(rng, 2), number_of)]


def centred(rng, shape, deviation, most, shards=(), held_as=jnp.bfloat16):
    result = deviation * jax.random.normal(rng, shape, jnp.float32)
    if shards:
        result = result * levels(rng, shape, shards, -0.22, 0.18)
    return jnp.clip(result, -most, most).astype(held_as)


def setup_inputs(seed: int = 0) -> dict:
    keys = jax.random.split(jax.random.key(seed), 11)
    hidden = centred(keys[0], (DOCS, L, D), 1.0, 6.0, ((0, 4), (1, 8)))
    span_lengths = jax.vmap(lambda own: ragged_sizes(own, NCH, L, SPAN_MAX, 2))(jax.random.split(keys[1], DOCS)).reshape((DOCS, NCH)).astype(jnp.int32)
    section_of = with_ends(skewed_ids(keys[2], (DOCS, NCH), NSEC, 2), jax.random.fold_in(keys[2], 3), 0, NSEC - 1).astype(jnp.int32)
    section_live = with_ends((jax.random.randint(keys[3], (NSEC,), 0, 4) < 3).astype(jnp.int32), jax.random.fold_in(keys[3], 1), 0, 1)
    w_in = centred(keys[4], (D, DS), (D // 64) ** -0.5, 0.5, ((0, 8),))
    norm_gain = jnp.clip(1.0 + 0.1 * jax.random.normal(keys[5], (DS,), jnp.float32), 0.5, 1.5)
    w_query = centred(keys[6], (DS, DS), DS ** -0.5, 0.125, ((1, 4),))
    w_key = centred(keys[7], (DS, DS), DS ** -0.5, 0.125, ((1, 4),))
    w_value = centred(keys[8], (DS, DS), DS ** -0.5, 0.125, ((1, 4),))
    w_out = centred(keys[9], (DS, DS), DS ** -0.5, 0.125, ((0, 4),))
    return {"hidden": hidden, "span_lengths": span_lengths, "section_of": section_of, "section_live": section_live, "w_in": w_in, "norm_gain": norm_gain, "w_query": w_query, "w_key": w_key, "w_value": w_value, "w_out": w_out}


def reference(hidden, span_lengths, section_of, section_live, w_in, norm_gain, w_query, w_key, w_value, w_out):
    span_ends = jnp.cumsum(span_lengths, axis=1).astype(jnp.int32)
    span_starts = (span_ends - span_lengths).astype(jnp.int32)
    positions = jnp.arange(L, dtype=jnp.int32)

    def pool_document(packed):
        tokens, starts, stops = packed
        member = ((positions[None, :] >= starts[:, None]) & (positions[None, :] < stops[:, None])).astype(jnp.bfloat16)
        return jnp.dot(member, tokens, preferred_element_type=jnp.float32)
    span_sums = lax.map(pool_document, (hidden, span_starts, span_ends))
    span_means = span_sums / span_lengths[:, :, None].astype(jnp.float32)
    flat_sections = section_of.reshape(-1)
    onehot = (jnp.arange(NSEC, dtype=jnp.int32)[:, None] == flat_sections[None, :]).astype(jnp.float32)
    section_sums = jnp.dot(onehot, span_means.reshape(-1, D), precision=lax.Precision.HIGHEST)
    section_count = lax.optimization_barrier(jnp.sum(onehot, axis=1))
    section_pooled = (section_sums / jnp.maximum(section_count, 1.0)[:, None]).astype(jnp.bfloat16)
    section_in = jnp.dot(section_pooled, w_in, preferred_element_type=jnp.float32)
    scale = lax.rsqrt(lax.optimization_barrier(jnp.mean(section_in * section_in, axis=1, keepdims=True)) + 1e-05)
    normed = (section_in * scale * norm_gain[None, :]).astype(jnp.bfloat16)
    queries = jnp.dot(normed, w_query, preferred_element_type=jnp.float32).astype(jnp.bfloat16)
    keys_all = jnp.dot(normed, w_key, preferred_element_type=jnp.float32).astype(jnp.bfloat16)
    values_all = jnp.dot(normed, w_value, preferred_element_type=jnp.float32).astype(jnp.bfloat16)
    query_heads = queries.reshape(NSEC, HEADS, HEAD_DIM).astype(jnp.float32)
    key_heads = keys_all.reshape(NSEC, HEADS, HEAD_DIM).astype(jnp.float32)
    value_heads = values_all.reshape(NSEC, HEADS, HEAD_DIM).astype(jnp.float32)
    scores = jnp.einsum('qhd,khd->hqk', query_heads, key_heads) / jnp.sqrt(jnp.float32(HEAD_DIM))
    section_ids = jnp.arange(NSEC, dtype=jnp.int32)
    allowed = (section_live[None, :] > 0) | (section_ids[None, :] == section_ids[:, None])
    scores = jnp.where(allowed[None, :, :], scores, jnp.float32(-1e+30))
    probs = jax.nn.softmax(scores, axis=-1).astype(jnp.bfloat16)
    attended = jnp.einsum('hqk,khd->qhd', probs.astype(jnp.float32), value_heads).astype(jnp.bfloat16)
    attended = attended.reshape(NSEC, DS)
    mixed = section_in + jnp.dot(attended, w_out, preferred_element_type=jnp.float32)
    return mixed.astype(jnp.bfloat16)
```

```python
import functools
import jax
import jax.numpy as jnp
from jax import lax
from jax.experimental import pallas as pl
from jax.experimental.pallas import tpu as pltpu
from jax.sharding import PartitionSpec as P

HEAD_DIM = 128
MESH = pl.DeviceIdType.MESH
IN_FLIGHT = 6


def chip_order(chip, chips):
    if chips & (chips - 1):
        return [(chip, lax.rem(chip + 1 + k, chips)) for k in range(chips)]
    order = []
    for mask in range(chips - 1, -1, -1):
        other, bit = chip, 1
        while bit < chips:
            if mask & bit:
                other = other + bit * (1 - 2 * lax.rem(lax.div(chip, bit), 2))
            bit *= 2
        order.append(other)
    return order


def kernel(
    seg_n, seq_n,
    hidden, lengths_in, sections_in, live_in, gain_in, w_in, w_query, w_key, w_value, w_out,
    out_ref,
    lengths_ref, sections_ref, live_ref, gain_ref, hid, win, wqkv, wout, weights,
    pair_send, pair_recv, line_send, line_recv, kept, product, proj_send, proj_recv, rows_all,
    kv_send, kv_recv, kv_all, term_recv,
    small_sem, load_sem, weight_sem, pair_ss, pair_rs, line_ss, line_rs,
    proj_ss, proj_rs, rows_ss, rows_rs, kv_ss, kv_rs, term_ss, term_rs,
):
    seg = lax.axis_index("segment")
    q = lax.axis_index("seq")
    core = lax.rem(q, 2)
    chip = lax.div(q, 2)
    chips = seq_n // 2
    partner = q + 1 - 2 * core
    tokens = hidden.shape[1]
    blocks, _, width = hid.shape
    parts = blocks // seq_n
    features = width * parts
    here = live_ref.shape[0]
    sections = here * seq_n
    docs, spans = lengths_ref.shape
    f32, bf16 = jnp.float32, jnp.bfloat16

    def seg_peer(d):
        return lax.rem(seg + d, seg_n)

    def seq_peer(d):
        return lax.rem(q + d, seq_n)

    others = chip_order(chip, chips)

    barrier = pltpu.get_barrier_semaphore()
    for d in range(1, seg_n):
        pl.semaphore_signal(barrier, inc=1, device_id=(seg_peer(d), q), device_id_type=MESH)
    for d in range(1, seq_n):
        pl.semaphore_signal(barrier, inc=1, device_id=(seg, seq_peer(d)), device_id_type=MESH)

    units = [(p, k) for p in range(parts) for k in range(chips - 1)] + [(p, chips - 1) for p in range(parts)]
    order = []
    for i, u in enumerate(units):
        order.append(("peer", u))
        if 1 <= i < len(units) - 1:
            order.append(("own", units[i - 1]))
    order += [("own", u) for u in units[-2:]]

    def load(i):
        kind, (p, k) = order[i]
        block = (others[k] * 2 + (core if kind == "own" else 1 - core)) * parts + p
        return pltpu.make_async_copy(
            hidden.at[0, :, pl.ds(pl.multiple_of(block * width, 128), width)],
            hid.at[i],
            load_sem.at[i],
        )

    small_loads = [
        pltpu.make_async_copy(source, target, small_sem.at[i])
        for i, (source, target) in enumerate((
            (lengths_in, lengths_ref), (sections_in, sections_ref),
            (live_in, live_ref), (gain_in, gain_ref)))
    ]
    weight_loads = [
        pltpu.make_async_copy(source, target, weight_sem.at[i])
        for i, (source, target) in enumerate((
            (w_in, win), (w_key, wqkv.at[1]), (w_value, wqkv.at[2]), (w_query, wqkv.at[0]),
            (w_out, wout)))
    ]
    for c in small_loads:
        c.start()
    for i in range(min(IN_FLIGHT, blocks)):
        load(i).start()
    for c in small_loads:
        c.wait()

    len_row = lengths_ref[pl.ds(seg, 1), :].astype(f32)
    sec_row = sections_ref[pl.ds(seg, 1), :]
    c_row = lax.broadcasted_iota(jnp.int32, (spans, spans), 0)
    c_col = lax.broadcasted_iota(jnp.int32, (spans, spans), 1)
    len_all = jnp.broadcast_to(len_row, (spans, spans))
    ends = jnp.sum(jnp.where(c_col <= c_row, len_all, 0.0), axis=1, keepdims=True)
    starts = jnp.sum(jnp.where(c_col < c_row, len_all, 0.0), axis=1, keepdims=True)
    position = (q * tokens + lax.broadcasted_iota(jnp.int32, (spans, tokens), 1)).astype(f32)
    member = jnp.where((position >= starts) & (position < ends), 1.0, 0.0).astype(bf16)
    s_row = lax.broadcasted_iota(jnp.int32, (sections, spans), 0)
    count = jnp.zeros((sections, 1), f32)
    for d in range(docs):
        same = s_row == sections_ref[d : d + 1, :]
        count += jnp.sum(jnp.where(same, 1.0, 0.0), axis=1, keepdims=True)
    share = jnp.where(s_row == sec_row, 1.0 / (len_row * jnp.maximum(count, 1.0)), 0.0)
    high = share.astype(bf16)
    low = (share - high.astype(f32)).astype(bf16)
    weights[...] = jnp.dot(
        jnp.concatenate([high, low], axis=0), member, preferred_element_type=f32
    ).astype(bf16)

    def pair_copy(p, k):
        return pltpu.make_async_remote_copy(
            pair_send.at[p, k], pair_recv.at[p, k], pair_ss, pair_rs.at[p, k],
            device_id=(seg, partner), device_id_type=MESH)

    def line_copy(p, k):
        return pltpu.make_async_remote_copy(
            line_send.at[p, k], line_recv.at[p, k], line_ss, line_rs.at[p],
            device_id=(seg, others[k] * 2 + core), device_id_type=MESH)

    def drain(ref, sem):
        pltpu.make_async_copy(ref, ref, sem).wait()

    ended = []
    ready = False
    for i, (kind, (p, k)) in enumerate(order):
        load(i).wait()
        if i + IN_FLIGHT < blocks:
            load(i + IN_FLIGHT).start()
        if i == blocks - 3:
            weight_loads[0].start()
        both = jnp.dot(weights[...], hid[i], preferred_element_type=f32)
        part = both[:sections] + both[sections:]
        if kind == "peer":
            pair_send[p, k] = part
            if not ready:
                pl.semaphore_wait(barrier, seg_n + seq_n - 2)
                ready = True
            pair_copy(p, k).start()
            continue
        pair_copy(p, k).wait_recv()
        part = part + pair_recv[p, k]
        if k < chips - 1:
            line_send[p, k] = part.astype(bf16)
            line_copy(p, k).start()
        else:
            kept[p] = part
    for w in weight_loads[1:]:
        w.start()
    ended += [(pair_send, pair_ss), (line_send, line_ss)]
    weight_loads[0].wait()
    for p in range(parts):
        drain(line_recv.at[p], line_rs.at[p])
        total = kept[p]
        for k in range(chips - 1):
            total += line_recv[p, k].astype(f32)
        term = jnp.dot(
            total.astype(bf16), win[p * width : (p + 1) * width, :], preferred_element_type=f32)
        if p:
            term = term + product[...]
        if p < parts - 1:
            product[...] = term
    for s in range(seq_n):
        proj_send[s] = term[s * here : (s + 1) * here, :].astype(bf16)

    def proj_copy(d):
        return pltpu.make_async_remote_copy(
            proj_send.at[seq_peer(d)], proj_recv.at[q], proj_ss, proj_rs,
            device_id=(seg, seq_peer(d)), device_id_type=MESH)

    far_first = []
    for k in range(chips - 1):
        for c in range(2):
            far_first.append(lax.rem(others[k] * 2 + c - q + seq_n, seq_n))
    far_first.append(lax.rem(partner - q + seq_n, seq_n))
    rest = pl.ds(0, seq_n - 1)
    for d in far_first:
        proj_copy(d).start()
    proj_recv[q] = proj_send[q]
    ended.append((proj_send.at[rest], proj_ss))
    drain(proj_recv.at[rest], proj_rs)
    partial = proj_recv[0].astype(f32)
    for s in range(1, seq_n):
        partial += proj_recv[s].astype(f32)
    rows_all[seg] = partial.astype(bf16)

    def rows_copy(d):
        return pltpu.make_async_remote_copy(
            rows_all.at[seg], rows_all.at[seg], rows_ss, rows_rs,
            device_id=(seg_peer(d), q), device_id_type=MESH)

    for d in range(1, seg_n):
        rows_copy(d).start()
    ended.append((rows_all.at[pl.ds(0, seg_n - 1)], rows_ss))
    drain(rows_all.at[pl.ds(0, seg_n - 1)], rows_rs)
    section_in = rows_all[0].astype(f32)
    for s in range(1, seg_n):
        section_in += rows_all[s].astype(f32)
    scale = lax.rsqrt(jnp.mean(section_in * section_in, axis=1, keepdims=True) + 1e-05)
    normed = (section_in * scale * gain_ref[...]).astype(bf16)
    columns = wqkv.shape[2]
    for w in weight_loads[1:]:
        w.wait()
    kv_send[:, 0:columns] = jnp.dot(normed, wqkv[1], preferred_element_type=f32).astype(bf16)
    kv_send[:, columns : 2 * columns] = jnp.dot(
        normed, wqkv[2], preferred_element_type=f32).astype(bf16)
    row = lax.broadcasted_iota(jnp.int32, (here, HEAD_DIM), 0)
    live = jnp.zeros((here, HEAD_DIM), f32)
    for i in range(here):
        live = jnp.where(row == i, live_ref[i].astype(f32), live)
    kv_send[:, 2 * columns :] = live.astype(bf16)

    def kv_copy(d):
        return pltpu.make_async_remote_copy(
            kv_send, kv_recv.at[q], kv_ss, kv_rs,
            device_id=(seg, seq_peer(d)), device_id_type=MESH)

    for d in far_first:
        kv_copy(d).start()
    kv_recv[q] = kv_send[...]
    ended.append((kv_recv.at[rest], kv_ss))
    queries = jnp.dot(normed, wqkv[0], preferred_element_type=f32).astype(bf16)
    drain(kv_recv.at[rest], kv_rs)
    for s in range(seq_n):
        kv_all[s * here : (s + 1) * here, :] = kv_recv[s].astype(f32)
    across = (((1,), (1,)), ((), ()))
    live_all = kv_all[:, 2 * columns :].astype(bf16)
    live_sum = lax.dot_general(
        jnp.ones((here, HEAD_DIM), bf16), live_all, across, preferred_element_type=f32)
    own = q * here + lax.broadcasted_iota(jnp.int32, (here, sections), 0)
    allowed = (live_sum > 0) | (lax.broadcasted_iota(jnp.int32, (here, sections), 1) == own)
    attended = []
    for h in range(columns // HEAD_DIM):
        lo = h * HEAD_DIM
        keys = kv_all[:, lo : lo + HEAD_DIM].astype(bf16)
        values = kv_all[:, columns + lo : columns + lo + HEAD_DIM].astype(bf16)
        scores = lax.dot_general(
            queries[:, lo : lo + HEAD_DIM], keys, across, preferred_element_type=f32)
        scores = jnp.where(allowed, scores / jnp.sqrt(f32(HEAD_DIM)), f32(-1e30))
        grown = jnp.exp(scores - jnp.max(scores, axis=1, keepdims=True))
        probs = (grown / jnp.sum(grown, axis=1, keepdims=True)).astype(bf16)
        attended.append(jnp.dot(probs, values, preferred_element_type=f32).astype(bf16))
    terms = jnp.dot(
        jnp.concatenate(attended, axis=1), wout[...], preferred_element_type=f32)
    term_recv[seg] = terms.astype(bf16)

    def term_copy(d):
        return pltpu.make_async_remote_copy(
            term_recv.at[seg], term_recv.at[seg], term_ss, term_rs,
            device_id=(seg_peer(d), q), device_id_type=MESH)

    for d in range(1, seg_n):
        term_copy(d).start()
    ended.append((term_recv.at[pl.ds(0, seg_n - 1)], term_ss))
    drain(term_recv.at[pl.ds(0, seg_n - 1)], term_rs)
    combined = term_recv[0].astype(f32)
    for s in range(1, seg_n):
        combined += term_recv[s].astype(f32)
    out_ref[...] = (section_in + combined).astype(out_ref.dtype)

    for ref, sem in ended:
        drain(ref, sem)


def shards(
    hidden, span_lengths, section_of, section_live, w_in, norm_gain, w_query, w_key, w_value, w_out
):
    seg_n, seq_n = lax.axis_size("segment"), lax.axis_size("seq")
    tokens, depth = hidden.shape[1:]
    here = section_live.shape[0]
    sections = here * seq_n
    chips = seq_n // 2
    features = depth // seq_n
    parts = max(features // 512, 1)
    block = features // parts
    width, columns = w_query.shape
    bf16, f32 = jnp.bfloat16, jnp.float32
    vmem = pl.BlockSpec(memory_space=pltpu.VMEM)
    hbm = pl.BlockSpec(memory_space=pl.ANY)
    dma = pltpu.SemaphoreType.DMA
    kv = 2 * columns + HEAD_DIM
    return pl.pallas_call(
        functools.partial(kernel, seg_n, seq_n),
        out_shape=jax.ShapeDtypeStruct((here, width), bf16),
        in_specs=[hbm] * 10,
        out_specs=vmem,
        scratch_shapes=[
            pltpu.VMEM(span_lengths.shape, jnp.int32),
            pltpu.VMEM(section_of.shape, jnp.int32),
            pltpu.SMEM((here,), jnp.int32),
            pltpu.VMEM((1, width), f32),
            pltpu.VMEM((seq_n * parts, tokens, block), bf16),
            pltpu.VMEM(w_in.shape, bf16),
            pltpu.VMEM((3, width, columns), bf16),
            pltpu.VMEM(w_out.shape, bf16),
            pltpu.VMEM((2 * sections, tokens), bf16),
            pltpu.VMEM((parts, chips, sections, block), f32),
            pltpu.VMEM((parts, chips, sections, block), f32),
            pltpu.VMEM((parts, chips - 1, sections, block), bf16),
            pltpu.VMEM((parts, chips - 1, sections, block), bf16),
            pltpu.VMEM((parts, sections, block), f32),
            pltpu.VMEM((sections, width), f32),
            pltpu.VMEM((seq_n, here, width), bf16),
            pltpu.VMEM((seq_n, here, width), bf16),
            pltpu.VMEM((seg_n, here, width), bf16),
            pltpu.VMEM((here, kv), bf16),
            pltpu.VMEM((seq_n, here, kv), bf16),
            pltpu.VMEM((sections, kv), f32),
            pltpu.VMEM((seg_n, here, width), bf16),
            dma((4,)), dma((seq_n * parts,)), dma((5,)),
            dma, dma((parts, chips)), dma, dma((parts,)),
            dma, dma, dma, dma, dma, dma, dma, dma,
        ],
        compiler_params=pltpu.CompilerParams(
            collective_id=0, has_side_effects=True, vmem_limit_bytes=60 * 1024 * 1024
        ),
    )(
        hidden, span_lengths, section_of, section_live, norm_gain.reshape(1, -1),
        w_in, w_query, w_key, w_value, w_out,
    )


def solution(mesh):
    in_specs = (
        P("segment", "seq", None),
        P(),
        P(),
        P("seq"),
        P("seq", None),
        P(),
        P(None, "segment"),
        P(None, "segment"),
        P(None, "segment"),
        P("segment", None),
    )
    out_specs = P("seq", None)
    return jax.shard_map(shards, mesh=mesh, in_specs=in_specs, out_specs=out_specs, check_vma=False)
```

```python
import functools
import jax
import jax.numpy as jnp
from jax import lax
from jax.experimental import pallas as pl
from jax.experimental.pallas import tpu as pltpu
from jax.sharding import PartitionSpec as P

HEAD_DIM = 128
MESH = pl.DeviceIdType.MESH
IN_FLIGHT = 6
LAG = 1
GREET = 0


def chip_order(chip, chips):
    if chips & (chips - 1):
        return [(chip, lax.rem(chip + 1 + k, chips)) for k in range(chips)]
    order = []
    for mask in range(chips - 1, -1, -1):
        other, bit = chip, 1
        while bit < chips:
            if mask & bit:
                other = other + bit * (1 - 2 * lax.rem(lax.div(chip, bit), 2))
            bit *= 2
        order.append(other)
    return order


def kernel(
    seg_n, seq_n, docs, spans, here,
    hidden, small, w_in, w_query, w_key, w_value, w_out,
    out_ref,
    hid, win, wqkv, wout, weights,
    pair_send, pair_recv, line_send, line_recv, kept, product, proj_send, proj_recv, rows_all,
    kv_send, kv_recv, kv_all, term_recv,
    load_sem, weight_sem, pair_ss, pair_rs, line_ss, line_rs,
    proj_ss, proj_rs, rows_ss, rows_rs, kv_ss, kv_rs, term_ss, term_rs,
):
    seg = lax.axis_index("segment")
    q = lax.axis_index("seq")
    core = lax.rem(q, 2)
    chip = lax.div(q, 2)
    chips = seq_n // 2
    partner = q + 1 - 2 * core
    tokens = hidden.shape[1]
    blocks, _, width = hid.shape
    parts = blocks // seq_n
    features = width * parts
    sections = here * seq_n
    f32, bf16 = jnp.float32, jnp.bfloat16

    def seg_peer(d):
        return lax.rem(seg + d, seg_n)

    def seq_peer(d):
        return lax.rem(q + d, seq_n)

    others = chip_order(chip, chips)

    barrier = pltpu.get_barrier_semaphore()
    for d in range(1, seg_n):
        pl.semaphore_signal(barrier, inc=1, device_id=(seg_peer(d), q), device_id_type=MESH)
    for d in range(1, seq_n):
        pl.semaphore_signal(barrier, inc=1, device_id=(seg, seq_peer(d)), device_id_type=MESH)

    units = [(p, k) for p in range(parts) for k in range(chips - 1)] + [(p, chips - 1) for p in range(parts)]
    order = [(kind, u) for u in units for kind in ("peer", "own")]

    def load(i):
        kind, (p, k) = order[i]
        block = (others[k] * 2 + (core if kind == "own" else 1 - core)) * parts + p
        return pltpu.make_async_copy(
            hidden.at[0, :, pl.ds(pl.multiple_of(block * width, 128), width)],
            hid.at[i],
            load_sem.at[i],
        )

    weight_loads = [
        pltpu.make_async_copy(source, target, weight_sem.at[i])
        for i, (source, target) in enumerate((
            (w_in, win), (w_key, wqkv.at[1]), (w_value, wqkv.at[2]), (w_query, wqkv.at[0]),
            (w_out, wout)))
    ]
    for i in range(min(IN_FLIGHT, blocks)):
        load(i).start()

    len_row = small[pl.ds(seg, 1), 0:spans]
    sec_row = small[pl.ds(docs + seg, 1), 0:spans]
    c_row = lax.broadcasted_iota(jnp.int32, (spans, spans), 0)
    c_col = lax.broadcasted_iota(jnp.int32, (spans, spans), 1)
    len_all = jnp.broadcast_to(len_row, (spans, spans))
    ends = jnp.sum(jnp.where(c_col <= c_row, len_all, 0.0), axis=1, keepdims=True)
    starts = jnp.sum(jnp.where(c_col < c_row, len_all, 0.0), axis=1, keepdims=True)
    position = (q * tokens + lax.broadcasted_iota(jnp.int32, (spans, tokens), 1)).astype(f32)
    member = jnp.where((position >= starts) & (position < ends), 1.0, 0.0).astype(bf16)
    s_row = lax.broadcasted_iota(jnp.int32, (sections, spans), 0).astype(f32)
    count = jnp.zeros((sections, 1), f32)
    for d in range(docs):
        same = s_row == small[docs + d : docs + d + 1, 0:spans]
        count += jnp.sum(jnp.where(same, 1.0, 0.0), axis=1, keepdims=True)
    share = jnp.where(s_row == sec_row, 1.0 / (len_row * jnp.maximum(count, 1.0)), 0.0)
    high = share.astype(bf16)
    low = (share - high.astype(f32)).astype(bf16)
    weights[...] = jnp.dot(
        jnp.concatenate([high, low], axis=0), member, preferred_element_type=f32
    ).astype(bf16)

    def pair_copy(p, k):
        return pltpu.make_async_remote_copy(
            pair_send.at[p, k], pair_recv.at[p, k], pair_ss, pair_rs.at[p, k],
            device_id=(seg, partner), device_id_type=MESH)

    def line_copy(p, k):
        return pltpu.make_async_remote_copy(
            line_send.at[p, k], line_recv.at[p, k], line_ss, line_rs.at[p],
            device_id=(seg, others[k] * 2 + core), device_id_type=MESH)

    def drain(ref, sem):
        pltpu.make_async_copy(ref, ref, sem).wait()

    def finish(p, k):
        pair_copy(p, k).wait_recv()
        part = kept[p, k] + pair_recv[p, k]
        if k < chips - 1:
            line_send[p, k] = part.astype(bf16)
            line_copy(p, k).start()
        else:
            kept[p, k] = part

    ended = []
    for i, (kind, (p, k)) in enumerate(order):
        load(i).wait()
        if i + IN_FLIGHT < blocks:
            load(i + IN_FLIGHT).start()
        if i == blocks - 3:
            weight_loads[0].start()
        both = jnp.dot(weights[...], hid[i], preferred_element_type=f32)
        part = both[:sections] + both[sections:]
        if kind == "own":
            kept[p, k] = part
            if i // 2 >= LAG:
                finish(*units[i // 2 - LAG])
            continue
        pair_send[p, k] = part
        if i // 2 == GREET:
            pl.semaphore_wait(barrier, seg_n + seq_n - 2)
            for u in units[:GREET]:
                pair_copy(*u).start()
        if i // 2 >= GREET:
            pair_copy(p, k).start()
    for u in units[len(units) - LAG :]:
        finish(*u)
    for w in weight_loads[1:]:
        w.start()
    ended += [(pair_send, pair_ss), (line_send, line_ss)]
    weight_loads[0].wait()
    for p in range(parts):
        drain(line_recv.at[p], line_rs.at[p])
        total = kept[p, chips - 1]
        for k in range(chips - 1):
            total += line_recv[p, k].astype(f32)
        term = jnp.dot(
            total.astype(bf16), win[p * width : (p + 1) * width, :], preferred_element_type=f32)
        if p:
            term = term + product[...]
        if p < parts - 1:
            product[...] = term
    for s in range(seq_n):
        proj_send[s] = term[s * here : (s + 1) * here, :].astype(bf16)

    def proj_copy(d):
        return pltpu.make_async_remote_copy(
            proj_send.at[seq_peer(d)], proj_recv.at[q], proj_ss, proj_rs,
            device_id=(seg, seq_peer(d)), device_id_type=MESH)

    far_first = []
    for k in range(chips - 1):
        for c in range(2):
            far_first.append(lax.rem(others[k] * 2 + c - q + seq_n, seq_n))
    far_first.append(lax.rem(partner - q + seq_n, seq_n))
    rest = pl.ds(0, seq_n - 1)
    for d in far_first:
        proj_copy(d).start()
    proj_recv[q] = proj_send[q]
    ended.append((proj_send.at[rest], proj_ss))
    drain(proj_recv.at[rest], proj_rs)
    partial = proj_recv[0].astype(f32)
    for s in range(1, seq_n):
        partial += proj_recv[s].astype(f32)
    rows_all[seg] = partial.astype(bf16)

    def rows_copy(d):
        return pltpu.make_async_remote_copy(
            rows_all.at[seg], rows_all.at[seg], rows_ss, rows_rs,
            device_id=(seg_peer(d), q), device_id_type=MESH)

    for d in range(1, seg_n):
        rows_copy(d).start()
    ended.append((rows_all.at[pl.ds(0, seg_n - 1)], rows_ss))
    drain(rows_all.at[pl.ds(0, seg_n - 1)], rows_rs)
    section_in = rows_all[0].astype(f32)
    for s in range(1, seg_n):
        section_in += rows_all[s].astype(f32)
    lanes = small.shape[1]
    first, rows = 2 * docs + 8, section_in.shape[1] // lanes
    scale = lax.rsqrt(jnp.mean(section_in * section_in, axis=1, keepdims=True) + 1e-05)
    normed = (section_in * scale * jnp.concatenate([small[i : i + 1, 0:lanes] for i in range(first, first + rows)], axis=1)).astype(bf16)
    columns = wqkv.shape[2]
    for w in weight_loads[1:]:
        w.wait()
    kv_send[:, 0:columns] = jnp.dot(normed, wqkv[1], preferred_element_type=f32).astype(bf16)
    kv_send[:, columns : 2 * columns] = jnp.dot(
        normed, wqkv[2], preferred_element_type=f32).astype(bf16)
    live_row = jnp.broadcast_to(small[2 * docs : 2 * docs + 1, 0:HEAD_DIM], (here, HEAD_DIM))
    on_diagonal = lax.broadcasted_iota(jnp.int32, (here, HEAD_DIM), 0) == lax.broadcasted_iota(
        jnp.int32, (here, HEAD_DIM), 1)
    live = jnp.sum(jnp.where(on_diagonal, live_row, 0.0), axis=1, keepdims=True)
    kv_send[:, 2 * columns :] = jnp.broadcast_to(live, (here, HEAD_DIM)).astype(bf16)

    def kv_copy(d):
        return pltpu.make_async_remote_copy(
            kv_send, kv_recv.at[q], kv_ss, kv_rs,
            device_id=(seg, seq_peer(d)), device_id_type=MESH)

    for d in far_first:
        kv_copy(d).start()
    kv_recv[q] = kv_send[...]
    ended.append((kv_recv.at[rest], kv_ss))
    queries = jnp.dot(normed, wqkv[0], preferred_element_type=f32).astype(bf16)
    drain(kv_recv.at[rest], kv_rs)
    for s in range(seq_n):
        kv_all[s * here : (s + 1) * here, :] = kv_recv[s].astype(f32)
    across = (((1,), (1,)), ((), ()))
    live_all = kv_all[:, 2 * columns :].astype(bf16)
    live_sum = lax.dot_general(
        jnp.ones((here, HEAD_DIM), bf16), live_all, across, preferred_element_type=f32)
    own = q * here + lax.broadcasted_iota(jnp.int32, (here, sections), 0)
    allowed = (live_sum > 0) | (lax.broadcasted_iota(jnp.int32, (here, sections), 1) == own)
    attended = []
    for h in range(columns // HEAD_DIM):
        lo = h * HEAD_DIM
        keys = kv_all[:, lo : lo + HEAD_DIM].astype(bf16)
        values = kv_all[:, columns + lo : columns + lo + HEAD_DIM].astype(bf16)
        scores = lax.dot_general(
            queries[:, lo : lo + HEAD_DIM], keys, across, preferred_element_type=f32)
        scores = jnp.where(allowed, scores / jnp.sqrt(f32(HEAD_DIM)), f32(-1e30))
        grown = jnp.exp(scores - jnp.max(scores, axis=1, keepdims=True))
        probs = (grown / jnp.sum(grown, axis=1, keepdims=True)).astype(bf16)
        attended.append(jnp.dot(probs, values, preferred_element_type=f32).astype(bf16))
    terms = jnp.dot(
        jnp.concatenate(attended, axis=1), wout[...], preferred_element_type=f32)
    term_recv[seg] = terms.astype(bf16)

    def term_copy(d):
        return pltpu.make_async_remote_copy(
            term_recv.at[seg], term_recv.at[seg], term_ss, term_rs,
            device_id=(seg_peer(d), q), device_id_type=MESH)

    for d in range(1, seg_n):
        term_copy(d).start()
    ended.append((term_recv.at[pl.ds(0, seg_n - 1)], term_ss))
    drain(term_recv.at[pl.ds(0, seg_n - 1)], term_rs)
    combined = term_recv[0].astype(f32)
    for s in range(1, seg_n):
        combined += term_recv[s].astype(f32)
    out_ref[...] = (section_in + combined).astype(out_ref.dtype)

    for ref, sem in ended:
        drain(ref, sem)


def shards(
    hidden, span_lengths, section_of, section_live, w_in, norm_gain, w_query, w_key, w_value, w_out
):
    seg_n, seq_n = lax.axis_size("segment"), lax.axis_size("seq")
    tokens, depth = hidden.shape[1:]
    docs, spans = span_lengths.shape
    lanes = max(128, spans)

    gains = norm_gain.reshape(-1, lanes)
    total_rows = 2 * docs + 8 + gains.shape[0]

    def padded(entries, row):
        return jnp.pad(
            entries, ((row, total_rows - row - entries.shape[0]), (0, lanes - entries.shape[1])))

    whole = (padded(span_lengths, 0) + padded(section_of, docs)) + padded(section_live.reshape(1, -1), 2 * docs)
    small = whole.astype(jnp.float32) + padded(gains, 2 * docs + 8)
    here = section_live.shape[0]
    sections = here * seq_n
    chips = seq_n // 2
    features = depth // seq_n
    parts = max(features // 512, 1)
    block = features // parts
    width, columns = w_query.shape
    bf16, f32 = jnp.bfloat16, jnp.float32
    vmem = pl.BlockSpec(memory_space=pltpu.VMEM)
    hbm = pl.BlockSpec(memory_space=pl.ANY)
    dma = pltpu.SemaphoreType.DMA
    kv = 2 * columns + HEAD_DIM
    return pl.pallas_call(
        functools.partial(kernel, seg_n, seq_n, docs, spans, here),
        out_shape=jax.ShapeDtypeStruct((here, width), bf16),
        in_specs=[hbm, vmem] + [hbm] * 5,
        out_specs=vmem,
        scratch_shapes=[
            pltpu.VMEM((seq_n * parts, tokens, block), bf16),
            pltpu.VMEM(w_in.shape, bf16),
            pltpu.VMEM((3, width, columns), bf16),
            pltpu.VMEM(w_out.shape, bf16),
            pltpu.VMEM((2 * sections, tokens), bf16),
            pltpu.VMEM((parts, chips, sections, block), f32),
            pltpu.VMEM((parts, chips, sections, block), f32),
            pltpu.VMEM((parts, chips - 1, sections, block), bf16),
            pltpu.VMEM((parts, chips - 1, sections, block), bf16),
            pltpu.VMEM((parts, chips, sections, block), f32),
            pltpu.VMEM((sections, width), f32),
            pltpu.VMEM((seq_n, here, width), bf16),
            pltpu.VMEM((seq_n, here, width), bf16),
            pltpu.VMEM((seg_n, here, width), bf16),
            pltpu.VMEM((here, kv), bf16),
            pltpu.VMEM((seq_n, here, kv), bf16),
            pltpu.VMEM((sections, kv), f32),
            pltpu.VMEM((seg_n, here, width), bf16),
            dma((seq_n * parts,)), dma((5,)),
            dma, dma((parts, chips)), dma, dma((parts,)),
            dma, dma, dma, dma, dma, dma, dma, dma,
        ],
        compiler_params=pltpu.CompilerParams(
            collective_id=0, has_side_effects=True, vmem_limit_bytes=53 * 1024 * 1024
        ),
    )(
        hidden, small, w_in, w_query, w_key, w_value, w_out,
    )


def solution(mesh):
    in_specs = (
        P("segment", "seq", None),
        P(),
        P(),
        P("seq"),
        P("seq", None),
        P(),
        P(None, "segment"),
        P(None, "segment"),
        P(None, "segment"),
        P("segment", None),
    )
    out_specs = P("seq", None)
    return jax.shard_map(shards, mesh=mesh, in_specs=in_specs, out_specs=out_specs, check_vma=False)
```

```python
import functools
import jax
import jax.numpy as jnp
from jax import lax
from jax.experimental import pallas as pl
from jax.experimental.pallas import tpu as pltpu
from jax.sharding import PartitionSpec as P

HEAD_DIM = 128
MESH = pl.DeviceIdType.MESH
IN_FLIGHT = 4
LAG = 1
HALVES = 1
GREET = 0


def chip_order(chip, chips):
    if chips & (chips - 1):
        return [(chip, lax.rem(chip + 1 + k, chips)) for k in range(chips)]
    order = []
    for mask in range(chips - 1, -1, -1):
        other, bit = chip, 1
        while bit < chips:
            if mask & bit:
                other = other + bit * (1 - 2 * lax.rem(lax.div(chip, bit), 2))
            bit *= 2
        order.append(other)
    return order


def kernel(
    seg_n, seq_n, docs, spans, here,
    hidden, small, w_in, w_query, w_key, w_value, w_out,
    out_ref,
    hid, win, wqkv, wout, weights,
    pair_send, pair_recv, line_send, line_recv, kept, product, proj_send, proj_recv, rows_all,
    key_send, key_recv, value_send, value_recv, kv_all, term_recv,
    load_sem, weight_sem, pair_ss, pair_rs, line_ss, line_rs,
    proj_ss, proj_rs, rows_ss, rows_rs, key_ss, key_rs, value_ss, value_rs, term_ss, term_rs,
):
    seg = lax.axis_index("segment")
    q = lax.axis_index("seq")
    core = lax.rem(q, 2)
    chip = lax.div(q, 2)
    chips = seq_n // 2
    partner = q + 1 - 2 * core
    tokens = hidden.shape[1]
    blocks, _, width = hid.shape
    parts = blocks // seq_n
    features = width * parts
    sections = here * seq_n
    f32, bf16 = jnp.float32, jnp.bfloat16

    def seg_peer(d):
        return lax.rem(seg + d, seg_n)

    def seq_peer(d):
        return lax.rem(q + d, seq_n)

    others = chip_order(chip, chips)

    units = [(p, k) for p in range(parts) for k in range(chips - 1)] + [(p, chips - 1) for p in range(parts)]
    order = [(kind, u) for u in units for kind in ("peer", "own")]

    def load(i):
        kind, (p, k) = order[i]
        block = (others[k] * 2 + (core if kind == "own" else 1 - core)) * parts + p
        return pltpu.make_async_copy(
            hidden.at[0, :, pl.ds(pl.multiple_of(block * width, 128), width)],
            hid.at[i],
            load_sem.at[i],
        )

    weight_loads = [
        pltpu.make_async_copy(source, target, weight_sem.at[i])
        for i, (source, target) in enumerate((
            (w_in, win), (w_key, wqkv.at[1]), (w_value, wqkv.at[2]), (w_query, wqkv.at[0]),
            (w_out, wout)))
    ]
    for i in range(min(IN_FLIGHT, blocks)):
        load(i).start()

    barrier = pltpu.get_barrier_semaphore()
    for d in range(1, seg_n):
        pl.semaphore_signal(barrier, inc=1, device_id=(seg_peer(d), q), device_id_type=MESH)
    for d in range(1, seq_n):
        pl.semaphore_signal(barrier, inc=1, device_id=(seg, seq_peer(d)), device_id_type=MESH)

    len_row = small[pl.ds(seg, 1), 0:spans]
    sec_row = small[pl.ds(docs + seg, 1), 0:spans]
    c_row = lax.broadcasted_iota(jnp.int32, (spans, spans), 0)
    c_col = lax.broadcasted_iota(jnp.int32, (spans, spans), 1)
    len_all = jnp.broadcast_to(len_row, (spans, spans))
    ends = jnp.sum(jnp.where(c_col <= c_row, len_all, 0.0), axis=1, keepdims=True)
    starts = jnp.sum(jnp.where(c_col < c_row, len_all, 0.0), axis=1, keepdims=True)
    position = (q * tokens + lax.broadcasted_iota(jnp.int32, (spans, tokens), 1)).astype(f32)
    member = jnp.where((position >= starts) & (position < ends), 1.0, 0.0).astype(bf16)
    s_row = lax.broadcasted_iota(jnp.int32, (sections, spans), 0).astype(f32)
    count = jnp.zeros((sections, 1), f32)
    for d in range(docs):
        same = s_row == small[docs + d : docs + d + 1, 0:spans]
        count += jnp.sum(jnp.where(same, 1.0, 0.0), axis=1, keepdims=True)
    share = jnp.where(s_row == sec_row, 1.0 / (len_row * jnp.maximum(count, 1.0)), 0.0)
    high = share.astype(bf16)
    low = (share - high.astype(f32)).astype(bf16)
    weights[...] = jnp.dot(
        jnp.concatenate([high, low], axis=0), member, preferred_element_type=f32
    ).astype(bf16)

    def pair_copy(p, k):
        return pltpu.make_async_remote_copy(
            pair_send.at[p, k], pair_recv.at[p, k], pair_ss, pair_rs.at[p, k],
            device_id=(seg, partner), device_id_type=MESH)

    def line_copy(p, k):
        return pltpu.make_async_remote_copy(
            line_send.at[p, k], line_recv.at[p, k], line_ss, line_rs.at[p],
            device_id=(seg, others[k] * 2 + core), device_id_type=MESH)

    def drain(ref, sem):
        pltpu.make_async_copy(ref, ref, sem).wait()

    def finish(p, k):
        pair_copy(p, k).wait_recv()
        part = kept[p, k] + pair_recv[p, k]
        if k < chips - 1:
            line_send[p, k] = part.astype(bf16)
            line_copy(p, k).start()
        else:
            kept[p, k] = part

    ended = []
    for i, (kind, (p, k)) in enumerate(order):
        load(i).wait()
        if i + IN_FLIGHT < blocks:
            load(i + IN_FLIGHT).start()
        if i == blocks - 3:
            weight_loads[0].start()
        both = jnp.dot(weights[...], hid[i], preferred_element_type=f32)
        part = both[:sections] + both[sections:]
        if kind == "own":
            kept[p, k] = part
            if i // 2 >= LAG:
                finish(*units[i // 2 - LAG])
            continue
        pair_send[p, k] = part
        if i // 2 == GREET:
            pl.semaphore_wait(barrier, seg_n + seq_n - 2)
            for u in units[:GREET]:
                pair_copy(*u).start()
        if i // 2 >= GREET:
            pair_copy(p, k).start()
    for u in units[len(units) - LAG :]:
        finish(*u)
    for w in weight_loads[1:]:
        w.start()
    ended += [(pair_send, pair_ss), (line_send, line_ss)]
    weight_loads[0].wait()
    depth = product.shape[1]
    half = depth // HALVES

    def proj_copy(d, n):
        cut = pl.ds(n * half, half)
        return pltpu.make_async_remote_copy(
            proj_send.at[seq_peer(d), :, cut], proj_recv.at[q, :, cut], proj_ss, proj_rs,
            device_id=(seg, seq_peer(d)), device_id_type=MESH)

    far_first = []
    for k in range(chips - 1):
        for c in range(2):
            far_first.append(lax.rem(others[k] * 2 + c - q + seq_n, seq_n))
    far_first.append(lax.rem(partner - q + seq_n, seq_n))
    rest = pl.ds(0, seq_n - 1)
    for p in range(parts):
        drain(line_recv.at[p], line_rs.at[p])
        total = kept[p, chips - 1]
        for k in range(chips - 1):
            total += line_recv[p, k].astype(f32)
        total = total.astype(bf16)
        for n in range(HALVES):
            cut = slice(n * half, (n + 1) * half)
            term = jnp.dot(total, win[p * width : (p + 1) * width, cut], preferred_element_type=f32)
            if p:
                term = term + product[:, cut]
            if p < parts - 1:
                product[:, cut] = term
                continue
            for s in range(seq_n):
                proj_send[s, :, cut] = term[s * here : (s + 1) * here, :].astype(bf16)
            for d in far_first:
                proj_copy(d, n).start()
    proj_recv[q] = proj_send[q]
    ended.append((proj_send.at[rest], proj_ss))
    drain(proj_recv.at[rest], proj_rs)
    partial = proj_recv[0].astype(f32)
    for s in range(1, seq_n):
        partial += proj_recv[s].astype(f32)
    rows_all[seg] = partial.astype(bf16)

    def rows_copy(d):
        return pltpu.make_async_remote_copy(
            rows_all.at[seg], rows_all.at[seg], rows_ss, rows_rs,
            device_id=(seg_peer(d), q), device_id_type=MESH)

    for d in range(1, seg_n):
        rows_copy(d).start()
    ended.append((rows_all.at[pl.ds(0, seg_n - 1)], rows_ss))
    drain(rows_all.at[pl.ds(0, seg_n - 1)], rows_rs)
    section_in = rows_all[0].astype(f32)
    for s in range(1, seg_n):
        section_in += rows_all[s].astype(f32)
    lanes = small.shape[1]
    first, rows = 2 * docs + 8, section_in.shape[1] // lanes
    scale = lax.rsqrt(jnp.mean(section_in * section_in, axis=1, keepdims=True) + 1e-05)
    normed = (section_in * scale * jnp.concatenate([small[i : i + 1, 0:lanes] for i in range(first, first + rows)], axis=1)).astype(bf16)
    columns = wqkv.shape[2]
    heads = columns // HEAD_DIM
    live_row = jnp.broadcast_to(small[2 * docs : 2 * docs + 1, 0:HEAD_DIM], (here, HEAD_DIM))
    on_diagonal = lax.broadcasted_iota(jnp.int32, (here, HEAD_DIM), 0) == lax.broadcasted_iota(
        jnp.int32, (here, HEAD_DIM), 1)
    live = jnp.sum(jnp.where(on_diagonal, live_row, 0.0), axis=1, keepdims=True)

    def spread_copy(source, target, send, receive, d):
        return pltpu.make_async_remote_copy(
            source, target.at[q], send, receive,
            device_id=(seg, seq_peer(d)), device_id_type=MESH)

    for w in weight_loads[1:]:
        w.wait()
    key_send[:, 0:columns] = jnp.dot(normed, wqkv[1], preferred_element_type=f32).astype(bf16)
    key_send[:, columns:] = jnp.broadcast_to(live, (here, HEAD_DIM)).astype(bf16)
    for d in far_first:
        spread_copy(key_send, key_recv, key_ss, key_rs, d).start()
    value_send[...] = jnp.dot(normed, wqkv[2], preferred_element_type=f32).astype(bf16)
    for d in far_first:
        spread_copy(value_send, value_recv, value_ss, value_rs, d).start()
    key_recv[q] = key_send[...]
    value_recv[q] = value_send[...]
    ended += [(key_recv.at[rest], key_ss), (value_recv.at[rest], value_ss)]
    stacked = heads * here
    own_head = lax.div(lax.broadcasted_iota(jnp.int32, (stacked, columns), 0), here) == lax.div(
        lax.broadcasted_iota(jnp.int32, (stacked, columns), 1), HEAD_DIM)
    queries = jnp.dot(normed, wqkv[0], preferred_element_type=f32)
    queries = jnp.where(own_head, jnp.concatenate([queries] * heads, axis=0), 0.0).astype(bf16)
    own = q * here + lax.rem(lax.broadcasted_iota(jnp.int32, (stacked, sections), 0), here)
    drain(key_recv.at[rest], key_rs)
    for s in range(seq_n):
        kv_all[s * here : (s + 1) * here, 0 : columns + HEAD_DIM] = key_recv[s].astype(f32)
    across = (((1,), (1,)), ((), ()))
    live_sum = lax.dot_general(
        jnp.ones((stacked, HEAD_DIM), bf16), kv_all[:, columns : columns + HEAD_DIM].astype(bf16), across,
        preferred_element_type=f32)
    allowed = (live_sum > 0) | (lax.broadcasted_iota(jnp.int32, (stacked, sections), 1) == own)
    scores = lax.dot_general(
        queries, kv_all[:, 0:columns].astype(bf16), across, preferred_element_type=f32)
    scores = jnp.where(allowed, scores / jnp.sqrt(f32(HEAD_DIM)), f32(-1e30))
    grown = jnp.exp(scores - jnp.max(scores, axis=1, keepdims=True))
    probs = (grown / jnp.sum(grown, axis=1, keepdims=True)).astype(bf16)
    drain(value_recv.at[rest], value_rs)
    for s in range(seq_n):
        kv_all[s * here : (s + 1) * here, columns + HEAD_DIM :] = value_recv[s].astype(f32)
    mixed = jnp.dot(probs, kv_all[:, columns + HEAD_DIM :].astype(bf16), preferred_element_type=f32)
    mixed = jnp.where(own_head, mixed, 0.0)
    attended = mixed[0:here]
    for h in range(1, heads):
        attended += mixed[h * here : (h + 1) * here]
    terms = jnp.dot(attended.astype(bf16), wout[...], preferred_element_type=f32)
    term_recv[seg] = terms.astype(bf16)

    def term_copy(d):
        return pltpu.make_async_remote_copy(
            term_recv.at[seg], term_recv.at[seg], term_ss, term_rs,
            device_id=(seg_peer(d), q), device_id_type=MESH)

    for d in range(1, seg_n):
        term_copy(d).start()
    ended.append((term_recv.at[pl.ds(0, seg_n - 1)], term_ss))
    drain(term_recv.at[pl.ds(0, seg_n - 1)], term_rs)
    combined = term_recv[0].astype(f32)
    for s in range(1, seg_n):
        combined += term_recv[s].astype(f32)
    out_ref[...] = (section_in + combined).astype(out_ref.dtype)

    for ref, sem in ended:
        drain(ref, sem)


def shards(
    hidden, span_lengths, section_of, section_live, w_in, norm_gain, w_query, w_key, w_value, w_out
):
    seg_n, seq_n = lax.axis_size("segment"), lax.axis_size("seq")
    tokens, depth = hidden.shape[1:]
    docs, spans = span_lengths.shape
    lanes = max(128, spans)

    gains = norm_gain.reshape(-1, lanes)
    total_rows = 2 * docs + 8 + gains.shape[0]

    def padded(entries, row):
        return jnp.pad(
            entries, ((row, total_rows - row - entries.shape[0]), (0, lanes - entries.shape[1])))

    whole = (padded(span_lengths, 0) + padded(section_of, docs)) + padded(section_live.reshape(1, -1), 2 * docs)
    small = whole.astype(jnp.float32) + padded(gains, 2 * docs + 8)
    here = section_live.shape[0]
    sections = here * seq_n
    chips = seq_n // 2
    features = depth // seq_n
    parts = max(features // 512, 1)
    block = features // parts
    width, columns = w_query.shape
    bf16, f32 = jnp.bfloat16, jnp.float32
    vmem = pl.BlockSpec(memory_space=pltpu.VMEM)
    hbm = pl.BlockSpec(memory_space=pl.ANY)
    dma = pltpu.SemaphoreType.DMA
    kv = 2 * columns + HEAD_DIM
    return pl.pallas_call(
        functools.partial(kernel, seg_n, seq_n, docs, spans, here),
        out_shape=jax.ShapeDtypeStruct((here, width), bf16),
        in_specs=[hbm, vmem] + [hbm] * 5,
        out_specs=vmem,
        scratch_shapes=[
            pltpu.VMEM((seq_n * parts, tokens, block), bf16),
            pltpu.VMEM(w_in.shape, bf16),
            pltpu.VMEM((3, width, columns), bf16),
            pltpu.VMEM(w_out.shape, bf16),
            pltpu.VMEM((2 * sections, tokens), bf16),
            pltpu.VMEM((parts, chips, sections, block), f32),
            pltpu.VMEM((parts, chips, sections, block), f32),
            pltpu.VMEM((parts, chips - 1, sections, block), bf16),
            pltpu.VMEM((parts, chips - 1, sections, block), bf16),
            pltpu.VMEM((parts, chips, sections, block), f32),
            pltpu.VMEM((sections, width), f32),
            pltpu.VMEM((seq_n, here, width), bf16),
            pltpu.VMEM((seq_n, here, width), bf16),
            pltpu.VMEM((seg_n, here, width), bf16),
            pltpu.VMEM((here, columns + HEAD_DIM), bf16),
            pltpu.VMEM((seq_n, here, columns + HEAD_DIM), bf16),
            pltpu.VMEM((here, columns), bf16),
            pltpu.VMEM((seq_n, here, columns), bf16),
            pltpu.VMEM((sections, kv), f32),
            pltpu.VMEM((seg_n, here, width), bf16),
            dma((seq_n * parts,)), dma((5,)),
            dma, dma((parts, chips)), dma, dma((parts,)),
            dma, dma, dma, dma, dma, dma, dma, dma, dma, dma,
        ],
        compiler_params=pltpu.CompilerParams(
            collective_id=0, has_side_effects=True, vmem_limit_bytes=53 * 1024 * 1024
        ),
    )(
        hidden, small, w_in, w_query, w_key, w_value, w_out,
    )


def solution(mesh):
    in_specs = (
        P("segment", "seq", None),
        P(),
        P(),
        P("seq"),
        P("seq", None),
        P(),
        P(None, "segment"),
        P(None, "segment"),
        P(None, "segment"),
        P("segment", None),
    )
    out_specs = P("seq", None)
    return jax.shard_map(shards, mesh=mesh, in_specs=in_specs, out_specs=out_specs, check_vma=False)
```

```python
import functools
import jax
import jax.numpy as jnp
from jax import lax
from jax.experimental import pallas as pl
from jax.experimental.pallas import tpu as pltpu
from jax.sharding import PartitionSpec as P

HEAD_DIM = 128
MESH = pl.DeviceIdType.MESH
IN_FLIGHT = 4
LAG = 1
HALVES = 1
GREET = 0


def chip_order(chip, chips):
    if chips & (chips - 1):
        return [(chip, lax.rem(chip + 1 + k, chips)) for k in range(chips)]
    order = []
    for mask in range(chips - 1, -1, -1):
        other, bit = chip, 1
        while bit < chips:
            if mask & bit:
                other = other + bit * (1 - 2 * lax.rem(lax.div(chip, bit), 2))
            bit *= 2
        order.append(other)
    return order


def kernel(
    seg_n, seq_n, docs, spans, here,
    hidden, small, w_in, w_query, w_key, w_value, w_out,
    out_ref,
    hid, win, wqkv, wout, weights,
    pair_send, pair_recv, line_send, line_recv, kept, product, proj_send, proj_recv, rows_all,
    key_send, key_recv, value_send, value_recv, kv_all, term_recv,
    load_sem, weight_sem, pair_ss, pair_rs, line_ss, line_rs,
    proj_ss, proj_rs, rows_ss, rows_rs, key_ss, key_rs, value_ss, value_rs, term_ss, term_rs,
):
    seg = lax.axis_index("segment")
    q = lax.axis_index("seq")
    core = lax.rem(q, 2)
    chip = lax.div(q, 2)
    chips = seq_n // 2
    partner = q + 1 - 2 * core
    tokens = hidden.shape[1]
    blocks, _, width = hid.shape
    parts = blocks // seq_n
    features = width * parts
    sections = here * seq_n
    f32, bf16 = jnp.float32, jnp.bfloat16

    seg_order = chip_order(seg, seg_n)[: seg_n - 1]

    def seg_peer(d):
        return seg_order[d - 1]

    def seq_peer(d):
        return lax.rem(q + d, seq_n)

    others = chip_order(chip, chips)

    units = [(p, k) for p in range(parts) for k in range(chips - 1)] + [(p, chips - 1) for p in range(parts)]
    order = [(kind, u) for u in units for kind in ("peer", "own")]

    def load(i):
        kind, (p, k) = order[i]
        block = (others[k] * 2 + (core if kind == "own" else 1 - core)) * parts + p
        return pltpu.make_async_copy(
            hidden.at[0, :, pl.ds(pl.multiple_of(block * width, 128), width)],
            hid.at[i],
            load_sem.at[i % IN_FLIGHT],
        )

    weight_loads = [
        pltpu.make_async_copy(source, target, weight_sem.at[min(i, 1)])
        for i, (source, target) in enumerate((
            (w_in, win), (w_key, wqkv.at[1]), (w_value, wqkv.at[2]), (w_query, wqkv.at[0]),
            (w_out, wout)))
    ]
    for i in range(min(IN_FLIGHT, blocks)):
        load(i).start()

    barrier = pltpu.get_barrier_semaphore()
    for d in range(1, seg_n):
        pl.semaphore_signal(barrier, inc=1, device_id=(seg_peer(d), q), device_id_type=MESH)
    for d in range(1, seq_n):
        pl.semaphore_signal(barrier, inc=1, device_id=(seg, seq_peer(d)), device_id_type=MESH)

    len_row = small[pl.ds(seg, 1), 0:spans]
    sec_row = small[pl.ds(docs + seg, 1), 0:spans]
    c_row = lax.broadcasted_iota(jnp.int32, (spans, spans), 0)
    c_col = lax.broadcasted_iota(jnp.int32, (spans, spans), 1)
    len_all = jnp.broadcast_to(len_row, (spans, spans))
    ends = jnp.sum(jnp.where(c_col <= c_row, len_all, 0.0), axis=1, keepdims=True)
    starts = jnp.sum(jnp.where(c_col < c_row, len_all, 0.0), axis=1, keepdims=True)
    position = (q * tokens + lax.broadcasted_iota(jnp.int32, (spans, tokens), 1)).astype(f32)
    member = jnp.where((position >= starts) & (position < ends), 1.0, 0.0).astype(bf16)
    s_row = lax.broadcasted_iota(jnp.int32, (sections, spans), 0).astype(f32)
    count = jnp.zeros((sections, 1), f32)
    for d in range(docs):
        same = s_row == small[docs + d : docs + d + 1, 0:spans]
        count += jnp.sum(jnp.where(same, 1.0, 0.0), axis=1, keepdims=True)
    share = jnp.where(s_row == sec_row, 1.0 / (len_row * jnp.maximum(count, 1.0)), 0.0)
    high = share.astype(bf16)
    low = (share - high.astype(f32)).astype(bf16)
    weights[...] = jnp.dot(
        jnp.concatenate([high, low], axis=0), member, preferred_element_type=f32
    ).astype(bf16)

    def pair_copy(p, k):
        return pltpu.make_async_remote_copy(
            pair_send.at[p, k], pair_recv.at[p, k], pair_ss, pair_rs.at[p, k],
            device_id=(seg, partner), device_id_type=MESH)

    def line_copy(p, k):
        return pltpu.make_async_remote_copy(
            line_send.at[p, k], line_recv.at[p, k], line_ss, line_rs.at[p],
            device_id=(seg, others[k] * 2 + core), device_id_type=MESH)

    def drain(ref, sem):
        pltpu.make_async_copy(ref, ref, sem).wait()

    def finish(p, k):
        pair_copy(p, k).wait_recv()
        part = kept[p, k] + pair_recv[p, k]
        if k < chips - 1:
            line_send[p, k] = part.astype(bf16)
            line_copy(p, k).start()
        else:
            kept[p, k] = part

    ended = []
    for i, (kind, (p, k)) in enumerate(order):
        load(i).wait()
        if i + IN_FLIGHT < blocks:
            load(i + IN_FLIGHT).start()
        if i == blocks - 3:
            weight_loads[0].start()
        both = jnp.dot(weights[...], hid[i], preferred_element_type=f32)
        part = both[:sections] + both[sections:]
        if kind == "own":
            kept[p, k] = part
            if i // 2 >= LAG:
                finish(*units[i // 2 - LAG])
            continue
        pair_send[p, k] = part
        if i // 2 == GREET:
            pl.semaphore_wait(barrier, seg_n + seq_n - 2)
            for u in units[:GREET]:
                pair_copy(*u).start()
        if i // 2 >= GREET:
            pair_copy(p, k).start()
    for u in units[len(units) - LAG :]:
        finish(*u)
    for w in weight_loads[1:]:
        w.start()
    ended += [(pair_send, pair_ss), (line_send, line_ss)]
    weight_loads[0].wait()
    depth = product.shape[1]
    half = depth // HALVES

    def proj_copy(d, n):
        cut = pl.ds(n * half, half)
        return pltpu.make_async_remote_copy(
            proj_send.at[seq_peer(d), :, cut], proj_recv.at[q, :, cut], proj_ss, proj_rs,
            device_id=(seg, seq_peer(d)), device_id_type=MESH)

    far_first = []
    for k in range(chips - 1):
        for c in range(2):
            far_first.append(lax.rem(others[k] * 2 + c - q + seq_n, seq_n))
    far_first.append(lax.rem(partner - q + seq_n, seq_n))
    rest = pl.ds(0, seq_n - 1)
    for p in range(parts):
        drain(line_recv.at[p], line_rs.at[p])
        total = kept[p, chips - 1]
        for k in range(chips - 1):
            total += line_recv[p, k].astype(f32)
        total = total.astype(bf16)
        for n in range(HALVES):
            cut = slice(n * half, (n + 1) * half)
            term = jnp.dot(total, win[p * width : (p + 1) * width, cut], preferred_element_type=f32)
            if p:
                term = term + product[:, cut]
            if p < parts - 1:
                product[:, cut] = term
                continue
            for s in range(seq_n):
                proj_send[s, :, cut] = term[s * here : (s + 1) * here, :].astype(bf16)
            for d in far_first:
                proj_copy(d, n).start()
    proj_recv[q] = proj_send[q]
    ended.append((proj_send.at[rest], proj_ss))
    drain(proj_recv.at[rest], proj_rs)
    partial = proj_recv[0].astype(f32)
    for s in range(1, seq_n):
        partial += proj_recv[s].astype(f32)
    rows_all[seg] = partial.astype(bf16)

    def rows_copy(d):
        return pltpu.make_async_remote_copy(
            rows_all.at[seg], rows_all.at[seg], rows_ss, rows_rs,
            device_id=(seg_peer(d), q), device_id_type=MESH)

    for d in range(1, seg_n):
        rows_copy(d).start()
    ended.append((rows_all.at[pl.ds(0, seg_n - 1)], rows_ss))
    drain(rows_all.at[pl.ds(0, seg_n - 1)], rows_rs)
    section_in = rows_all[0].astype(f32)
    for s in range(1, seg_n):
        section_in += rows_all[s].astype(f32)
    lanes = small.shape[1]
    first, rows = 2 * docs + 8, section_in.shape[1] // lanes
    scale = lax.rsqrt(jnp.mean(section_in * section_in, axis=1, keepdims=True) + 1e-05)
    normed = (section_in * scale * jnp.concatenate([small[i : i + 1, 0:lanes] for i in range(first, first + rows)], axis=1)).astype(bf16)
    columns = wqkv.shape[2]
    heads = columns // HEAD_DIM
    live_row = jnp.broadcast_to(small[2 * docs : 2 * docs + 1, 0:HEAD_DIM], (here, HEAD_DIM))
    on_diagonal = lax.broadcasted_iota(jnp.int32, (here, HEAD_DIM), 0) == lax.broadcasted_iota(
        jnp.int32, (here, HEAD_DIM), 1)
    live = jnp.sum(jnp.where(on_diagonal, live_row, 0.0), axis=1, keepdims=True)

    def spread_copy(source, target, send, receive, d):
        return pltpu.make_async_remote_copy(
            source, target.at[q], send, receive,
            device_id=(seg, seq_peer(d)), device_id_type=MESH)

    drain(wqkv, weight_sem.at[1])
    drain(wout, weight_sem.at[1])
    key_send[:, 0:columns] = jnp.dot(normed, wqkv[1], preferred_element_type=f32).astype(bf16)
    key_send[:, columns:] = jnp.broadcast_to(live, (here, HEAD_DIM)).astype(bf16)
    for d in far_first:
        spread_copy(key_send, key_recv, key_ss, key_rs, d).start()
    value_send[...] = jnp.dot(normed, wqkv[2], preferred_element_type=f32).astype(bf16)
    for d in far_first:
        spread_copy(value_send, value_recv, value_ss, value_rs, d).start()
    key_recv[q] = key_send[...]
    value_recv[q] = value_send[...]
    ended += [(key_recv.at[rest], key_ss), (value_recv.at[rest], value_ss)]
    stacked = heads * here
    own_head = lax.div(lax.broadcasted_iota(jnp.int32, (stacked, columns), 0), here) == lax.div(
        lax.broadcasted_iota(jnp.int32, (stacked, columns), 1), HEAD_DIM)
    queries = jnp.dot(normed, wqkv[0], preferred_element_type=f32)
    queries = jnp.where(own_head, jnp.concatenate([queries] * heads, axis=0), 0.0).astype(bf16)
    own = q * here + lax.rem(lax.broadcasted_iota(jnp.int32, (stacked, sections), 0), here)
    drain(key_recv.at[rest], key_rs)
    for s in range(seq_n):
        kv_all[s * here : (s + 1) * here, 0 : columns + HEAD_DIM] = key_recv[s].astype(f32)
    across = (((1,), (1,)), ((), ()))
    live_sum = lax.dot_general(
        jnp.ones((stacked, HEAD_DIM), bf16), kv_all[:, columns : columns + HEAD_DIM].astype(bf16), across,
        preferred_element_type=f32)
    allowed = (live_sum > 0) | (lax.broadcasted_iota(jnp.int32, (stacked, sections), 1) == own)
    scores = lax.dot_general(
        queries, kv_all[:, 0:columns].astype(bf16), across, preferred_element_type=f32)
    scores = jnp.where(allowed, scores / jnp.sqrt(f32(HEAD_DIM)), f32(-1e30))
    grown = jnp.exp(scores - jnp.max(scores, axis=1, keepdims=True))
    probs = (grown / jnp.sum(grown, axis=1, keepdims=True)).astype(bf16)
    drain(value_recv.at[rest], value_rs)
    for s in range(seq_n):
        kv_all[s * here : (s + 1) * here, columns + HEAD_DIM :] = value_recv[s].astype(f32)
    mixed = jnp.dot(probs, kv_all[:, columns + HEAD_DIM :].astype(bf16), preferred_element_type=f32)
    mixed = jnp.where(own_head, mixed, 0.0)
    attended = mixed[0:here]
    for h in range(1, heads):
        attended += mixed[h * here : (h + 1) * here]
    terms = jnp.dot(attended.astype(bf16), wout[...], preferred_element_type=f32)
    term_recv[seg] = terms.astype(bf16)

    def term_copy(d):
        return pltpu.make_async_remote_copy(
            term_recv.at[seg], term_recv.at[seg], term_ss, term_rs,
            device_id=(seg_peer(d), q), device_id_type=MESH)

    for d in range(1, seg_n):
        term_copy(d).start()
    ended.append((term_recv.at[pl.ds(0, seg_n - 1)], term_ss))
    drain(term_recv.at[pl.ds(0, seg_n - 1)], term_rs)
    combined = term_recv[0].astype(f32)
    for s in range(1, seg_n):
        combined += term_recv[s].astype(f32)
    out_ref[...] = (section_in + combined).astype(out_ref.dtype)

    for ref, sem in ended:
        drain(ref, sem)


def shards(
    hidden, span_lengths, section_of, section_live, w_in, norm_gain, w_query, w_key, w_value, w_out
):
    seg_n, seq_n = lax.axis_size("segment"), lax.axis_size("seq")
    tokens, depth = hidden.shape[1:]
    docs, spans = span_lengths.shape
    lanes = max(128, spans)

    gains = norm_gain.reshape(-1, lanes)
    total_rows = 2 * docs + 8 + gains.shape[0]

    def padded(entries, row):
        return jnp.pad(
            entries, ((row, total_rows - row - entries.shape[0]), (0, lanes - entries.shape[1])))

    whole = (padded(span_lengths, 0) + padded(section_of, docs)) + padded(section_live.reshape(1, -1), 2 * docs)
    small = whole.astype(jnp.float32) + padded(gains, 2 * docs + 8)
    here = section_live.shape[0]
    sections = here * seq_n
    chips = seq_n // 2
    features = depth // seq_n
    parts = max(features // 512, 1)
    block = features // parts
    width, columns = w_query.shape
    bf16, f32 = jnp.bfloat16, jnp.float32
    vmem = pl.BlockSpec(memory_space=pltpu.VMEM)
    hbm = pl.BlockSpec(memory_space=pl.ANY)
    dma = pltpu.SemaphoreType.DMA
    kv = 2 * columns + HEAD_DIM
    return pl.pallas_call(
        functools.partial(kernel, seg_n, seq_n, docs, spans, here),
        out_shape=jax.ShapeDtypeStruct((here, width), bf16),
        in_specs=[hbm, vmem] + [hbm] * 5,
        out_specs=vmem,
        scratch_shapes=[
            pltpu.VMEM((seq_n * parts, tokens, block), bf16),
            pltpu.VMEM(w_in.shape, bf16),
            pltpu.VMEM((3, width, columns), bf16),
            pltpu.VMEM(w_out.shape, bf16),
            pltpu.VMEM((2 * sections, tokens), bf16),
            pltpu.VMEM((parts, chips, sections, block), f32),
            pltpu.VMEM((parts, chips, sections, block), f32),
            pltpu.VMEM((parts, chips - 1, sections, block), bf16),
            pltpu.VMEM((parts, chips - 1, sections, block), bf16),
            pltpu.VMEM((parts, chips, sections, block), f32),
            pltpu.VMEM((sections, width), f32),
            pltpu.VMEM((seq_n, here, width), bf16),
            pltpu.VMEM((seq_n, here, width), bf16),
            pltpu.VMEM((seg_n, here, width), bf16),
            pltpu.VMEM((here, columns + HEAD_DIM), bf16),
            pltpu.VMEM((seq_n, here, columns + HEAD_DIM), bf16),
            pltpu.VMEM((here, columns), bf16),
            pltpu.VMEM((seq_n, here, columns), bf16),
            pltpu.VMEM((sections, kv), f32),
            pltpu.VMEM((seg_n, here, width), bf16),
            dma((IN_FLIGHT,)), dma((2,)),
            dma, dma((parts, chips)), dma, dma((parts,)),
            dma, dma, dma, dma, dma, dma, dma, dma, dma, dma,
        ],
        compiler_params=pltpu.CompilerParams(
            collective_id=0, has_side_effects=True, vmem_limit_bytes=53 * 1024 * 1024
        ),
    )(
        hidden, small, w_in, w_query, w_key, w_value, w_out,
    )


def solution(mesh):
    in_specs = (
        P("segment", "seq", None),
        P(),
        P(),
        P("seq"),
        P("seq", None),
        P(),
        P(None, "segment"),
        P(None, "segment"),
        P(None, "segment"),
        P("segment", None),
    )
    out_specs = P("seq", None)
    return jax.shard_map(shards, mesh=mesh, in_specs=in_specs, out_specs=out_specs, check_vma=False)
```

```python
import functools
import jax
import jax.numpy as jnp
from jax import lax
from jax.experimental import pallas as pl
from jax.experimental.pallas import tpu as pltpu
from jax.sharding import PartitionSpec as P

HEAD_DIM = 128
MESH = pl.DeviceIdType.MESH
IN_FLIGHT = 4
LAG = 1
HALVES = 1
GREET = 0


def chip_order(chip, chips):
    if chips & (chips - 1):
        return [(chip, lax.rem(chip + 1 + k, chips)) for k in range(chips)]
    order = []
    for mask in range(chips - 1, -1, -1):
        other, bit = chip, 1
        while bit < chips:
            if mask & bit:
                other = other + bit * (1 - 2 * lax.rem(lax.div(chip, bit), 2))
            bit *= 2
        order.append(other)
    return order


def kernel(
    seg_n, seq_n, docs, spans, here,
    hidden, small, w_in, w_query, w_key, w_value, w_out,
    out_ref,
    hid, win, wqkv, wout, weights,
    pair_send, pair_recv, line_send, line_recv, kept, product, proj_send, proj_recv, rows_all,
    key_send, key_recv, value_send, value_recv, kv_all, term_recv,
    load_sem, weight_sem, pair_ss, pair_rs, line_ss, line_rs,
    proj_ss, proj_rs, rows_ss, rows_rs, key_ss, key_rs, value_ss, value_rs, term_ss, term_rs,
):
    seg = lax.axis_index("segment")
    q = lax.axis_index("seq")
    core = lax.rem(q, 2)
    chip = lax.div(q, 2)
    chips = seq_n // 2
    partner = q + 1 - 2 * core
    tokens = hidden.shape[1]
    blocks, _, width = hid.shape
    parts = blocks // seq_n
    features = width * parts
    sections = here * seq_n
    f32, bf16 = jnp.float32, jnp.bfloat16

    seg_order = chip_order(seg, seg_n)[: seg_n - 1]

    def seg_peer(d):
        return seg_order[d - 1]

    def seq_peer(d):
        return lax.rem(q + d, seq_n)

    others = chip_order(chip, chips)

    units = [(p, k) for p in range(parts) for k in range(chips - 1)] + [(p, chips - 1) for p in range(parts)]
    order = [("peer", units[0])]
    for i in range(1, len(units)):
        order += [("peer", units[i]), ("own", units[i - 1])]
    order.append(("own", units[-1]))

    def load(i):
        kind, (p, k) = order[i]
        block = (others[k] * 2 + (core if kind == "own" else 1 - core)) * parts + p
        return pltpu.make_async_copy(
            hidden.at[0, :, pl.ds(pl.multiple_of(block * width, 128), width)],
            hid.at[i],
            load_sem.at[i % IN_FLIGHT],
        )

    weight_loads = [
        pltpu.make_async_copy(source, target, weight_sem.at[min(i, 1)])
        for i, (source, target) in enumerate((
            (w_in, win), (w_key, wqkv.at[1]), (w_value, wqkv.at[2]), (w_query, wqkv.at[0]),
            (w_out, wout)))
    ]
    for i in range(min(IN_FLIGHT, blocks)):
        load(i).start()

    barrier = pltpu.get_barrier_semaphore()
    for d in range(1, seg_n):
        pl.semaphore_signal(barrier, inc=1, device_id=(seg_peer(d), q), device_id_type=MESH)
    for d in range(1, seq_n):
        pl.semaphore_signal(barrier, inc=1, device_id=(seg, seq_peer(d)), device_id_type=MESH)

    len_row = small[pl.ds(seg, 1), 0:spans]
    sec_row = small[pl.ds(docs + seg, 1), 0:spans]
    c_row = lax.broadcasted_iota(jnp.int32, (spans, spans), 0)
    c_col = lax.broadcasted_iota(jnp.int32, (spans, spans), 1)
    len_all = jnp.broadcast_to(len_row, (spans, spans))
    ends = jnp.sum(jnp.where(c_col <= c_row, len_all, 0.0), axis=1, keepdims=True)
    starts = jnp.sum(jnp.where(c_col < c_row, len_all, 0.0), axis=1, keepdims=True)
    position = (q * tokens + lax.broadcasted_iota(jnp.int32, (spans, tokens), 1)).astype(f32)
    member = jnp.where((position >= starts) & (position < ends), 1.0, 0.0).astype(bf16)
    s_row = lax.broadcasted_iota(jnp.int32, (sections, spans), 0).astype(f32)
    count = jnp.zeros((sections, 1), f32)
    for d in range(docs):
        same = s_row == small[docs + d : docs + d + 1, 0:spans]
        count += jnp.sum(jnp.where(same, 1.0, 0.0), axis=1, keepdims=True)
    share = jnp.where(s_row == sec_row, 1.0 / (len_row * jnp.maximum(count, 1.0)), 0.0)
    high = share.astype(bf16)
    low = (share - high.astype(f32)).astype(bf16)
    weights[...] = jnp.dot(
        jnp.concatenate([high, low], axis=0), member, preferred_element_type=f32
    ).astype(bf16)

    def pair_copy(p, k):
        return pltpu.make_async_remote_copy(
            pair_send.at[p, k], pair_recv.at[p, k], pair_ss, pair_rs.at[p, k],
            device_id=(seg, partner), device_id_type=MESH)

    def line_copy(p, k):
        return pltpu.make_async_remote_copy(
            line_send.at[p, k], line_recv.at[p, k], line_ss, line_rs.at[p],
            device_id=(seg, others[k] * 2 + core), device_id_type=MESH)

    def drain(ref, sem):
        pltpu.make_async_copy(ref, ref, sem).wait()

    def finish(p, k):
        pair_copy(p, k).wait_recv()
        part = kept[p, k] + pair_recv[p, k]
        if k < chips - 1:
            line_send[p, k] = part.astype(bf16)
            line_copy(p, k).start()
        else:
            kept[p, k] = part

    ended = []
    for i, (kind, (p, k)) in enumerate(order):
        load(i).wait()
        if i + IN_FLIGHT < blocks:
            load(i + IN_FLIGHT).start()
        if i == blocks - 3:
            weight_loads[0].start()
        both = jnp.dot(weights[...], hid[i], preferred_element_type=f32)
        part = both[:sections] + both[sections:]
        if kind == "own":
            kept[p, k] = part
            if k < chips - 1:
                finish(p, k)
            continue
        pair_send[p, k] = part
        if i == 0:
            pl.semaphore_wait(barrier, seg_n + seq_n - 2)
        pair_copy(p, k).start()
    for p in range(parts):
        finish(p, chips - 1)
    ended += [(pair_send, pair_ss), (line_send, line_ss)]
    weight_loads[0].wait()
    for w in weight_loads[1:]:
        w.start()
    depth = product.shape[1]
    half = depth // HALVES

    def proj_copy(d, n):
        cut = pl.ds(n * half, half)
        return pltpu.make_async_remote_copy(
            proj_send.at[seq_peer(d), :, cut], proj_recv.at[q, :, cut], proj_ss, proj_rs,
            device_id=(seg, seq_peer(d)), device_id_type=MESH)

    far_first = []
    for k in range(chips - 1):
        for c in range(2):
            far_first.append(lax.rem(others[k] * 2 + c - q + seq_n, seq_n))
    far_first.append(lax.rem(partner - q + seq_n, seq_n))
    rest = pl.ds(0, seq_n - 1)
    for p in range(parts):
        drain(line_recv.at[p], line_rs.at[p])
        total = kept[p, chips - 1]
        for k in range(chips - 1):
            total += line_recv[p, k].astype(f32)
        total = total.astype(bf16)
        for n in range(HALVES):
            cut = slice(n * half, (n + 1) * half)
            term = jnp.dot(total, win[p * width : (p + 1) * width, cut], preferred_element_type=f32)
            if p:
                term = term + product[:, cut]
            if p < parts - 1:
                product[:, cut] = term
                continue
            for s in range(seq_n):
                proj_send[s, :, cut] = term[s * here : (s + 1) * here, :].astype(bf16)
            for d in far_first:
                proj_copy(d, n).start()
    proj_recv[q] = proj_send[q]
    ended.append((proj_send.at[rest], proj_ss))
    drain(proj_recv.at[rest], proj_rs)
    partial = proj_recv[0].astype(f32)
    for s in range(1, seq_n):
        partial += proj_recv[s].astype(f32)
    rows_all[seg] = partial.astype(bf16)

    def rows_copy(d):
        return pltpu.make_async_remote_copy(
            rows_all.at[seg], rows_all.at[seg], rows_ss, rows_rs,
            device_id=(seg_peer(d), q), device_id_type=MESH)

    for d in range(1, seg_n):
        rows_copy(d).start()
    ended.append((rows_all.at[pl.ds(0, seg_n - 1)], rows_ss))
    drain(rows_all.at[pl.ds(0, seg_n - 1)], rows_rs)
    section_in = rows_all[0].astype(f32)
    for s in range(1, seg_n):
        section_in += rows_all[s].astype(f32)
    lanes = small.shape[1]
    first, rows = 2 * docs + 8, section_in.shape[1] // lanes
    scale = lax.rsqrt(jnp.mean(section_in * section_in, axis=1, keepdims=True) + 1e-05)
    normed = (section_in * jnp.concatenate([small[i : i + 1, 0:lanes] for i in range(first, first + rows)], axis=1)).astype(bf16)
    columns = wqkv.shape[2]
    heads = columns // HEAD_DIM
    live_row = jnp.broadcast_to(small[2 * docs : 2 * docs + 1, 0:HEAD_DIM], (here, HEAD_DIM))
    on_diagonal = lax.broadcasted_iota(jnp.int32, (here, HEAD_DIM), 0) == lax.broadcasted_iota(
        jnp.int32, (here, HEAD_DIM), 1)
    live = jnp.sum(jnp.where(on_diagonal, live_row, 0.0), axis=1, keepdims=True)

    def spread_copy(source, target, send, receive, d):
        return pltpu.make_async_remote_copy(
            source, target.at[q], send, receive,
            device_id=(seg, seq_peer(d)), device_id_type=MESH)

    drain(wqkv, weight_sem.at[1])
    drain(wout, weight_sem.at[1])
    key_send[:, 0:columns] = (scale * jnp.dot(normed, wqkv[1], preferred_element_type=f32)).astype(bf16)
    key_send[:, columns:] = jnp.broadcast_to(live, (here, HEAD_DIM)).astype(bf16)
    for d in far_first:
        spread_copy(key_send, key_recv, key_ss, key_rs, d).start()
    value_send[...] = (scale * jnp.dot(normed, wqkv[2], preferred_element_type=f32)).astype(bf16)
    for d in far_first:
        spread_copy(value_send, value_recv, value_ss, value_rs, d).start()
    key_recv[q] = key_send[...]
    value_recv[q] = value_send[...]
    ended += [(key_recv.at[rest], key_ss), (value_recv.at[rest], value_ss)]
    stacked = heads * here
    own_head = lax.div(lax.broadcasted_iota(jnp.int32, (stacked, columns), 0), here) == lax.div(
        lax.broadcasted_iota(jnp.int32, (stacked, columns), 1), HEAD_DIM)
    queries = scale * jnp.dot(normed, wqkv[0], preferred_element_type=f32)
    queries = jnp.where(own_head, jnp.concatenate([queries] * heads, axis=0), 0.0).astype(bf16)
    own = q * here + lax.rem(lax.broadcasted_iota(jnp.int32, (stacked, sections), 0), here)
    drain(key_recv.at[rest], key_rs)
    for s in range(seq_n):
        kv_all[s * here : (s + 1) * here, 0 : columns + HEAD_DIM] = key_recv[s].astype(f32)
    across = (((1,), (1,)), ((), ()))
    live_sum = lax.dot_general(
        jnp.ones((stacked, HEAD_DIM), bf16), kv_all[:, columns : columns + HEAD_DIM].astype(bf16), across,
        preferred_element_type=f32)
    allowed = (live_sum > 0) | (lax.broadcasted_iota(jnp.int32, (stacked, sections), 1) == own)
    scores = lax.dot_general(
        queries, kv_all[:, 0:columns].astype(bf16), across, preferred_element_type=f32)
    scores = jnp.where(allowed, scores / jnp.sqrt(f32(HEAD_DIM)), f32(-1e30))
    grown = jnp.exp(scores - jnp.max(scores, axis=1, keepdims=True))
    probs = (grown / jnp.sum(grown, axis=1, keepdims=True)).astype(bf16)
    drain(value_recv.at[rest], value_rs)
    for s in range(seq_n):
        kv_all[s * here : (s + 1) * here, columns + HEAD_DIM :] = value_recv[s].astype(f32)
    mixed = jnp.dot(probs, kv_all[:, columns + HEAD_DIM :].astype(bf16), preferred_element_type=f32)
    mixed = jnp.where(own_head, mixed, 0.0)
    attended = mixed[0:here]
    for h in range(1, heads):
        attended += mixed[h * here : (h + 1) * here]
    terms = jnp.dot(attended.astype(bf16), wout[...], preferred_element_type=f32)
    term_recv[seg] = terms.astype(bf16)

    def term_copy(d):
        return pltpu.make_async_remote_copy(
            term_recv.at[seg], term_recv.at[seg], term_ss, term_rs,
            device_id=(seg_peer(d), q), device_id_type=MESH)

    for d in range(1, seg_n):
        term_copy(d).start()
    ended.append((term_recv.at[pl.ds(0, seg_n - 1)], term_ss))
    drain(term_recv.at[pl.ds(0, seg_n - 1)], term_rs)
    combined = term_recv[0].astype(f32)
    for s in range(1, seg_n):
        combined += term_recv[s].astype(f32)
    out_ref[...] = (section_in + combined).astype(out_ref.dtype)

    for ref, sem in ended:
        drain(ref, sem)


def shards(
    hidden, span_lengths, section_of, section_live, w_in, norm_gain, w_query, w_key, w_value, w_out
):
    seg_n, seq_n = lax.axis_size("segment"), lax.axis_size("seq")
    tokens, depth = hidden.shape[1:]
    docs, spans = span_lengths.shape
    lanes = max(128, spans)

    gains = norm_gain.reshape(-1, lanes)
    total_rows = 2 * docs + 8 + gains.shape[0]

    def padded(entries, row):
        return jnp.pad(
            entries, ((row, total_rows - row - entries.shape[0]), (0, lanes - entries.shape[1])))

    whole = (padded(span_lengths, 0) + padded(section_of, docs)) + padded(section_live.reshape(1, -1), 2 * docs)
    small = whole.astype(jnp.float32) + padded(gains, 2 * docs + 8)
    here = section_live.shape[0]
    sections = here * seq_n
    chips = seq_n // 2
    features = depth // seq_n
    parts = max(features // 512, 1)
    block = features // parts
    width, columns = w_query.shape
    bf16, f32 = jnp.bfloat16, jnp.float32
    vmem = pl.BlockSpec(memory_space=pltpu.VMEM)
    hbm = pl.BlockSpec(memory_space=pl.ANY)
    dma = pltpu.SemaphoreType.DMA
    kv = 2 * columns + HEAD_DIM
    return pl.pallas_call(
        functools.partial(kernel, seg_n, seq_n, docs, spans, here),
        out_shape=jax.ShapeDtypeStruct((here, width), bf16),
        in_specs=[hbm, vmem] + [hbm] * 5,
        out_specs=vmem,
        scratch_shapes=[
            pltpu.VMEM((seq_n * parts, tokens, block), bf16),
            pltpu.VMEM(w_in.shape, bf16),
            pltpu.VMEM((3, width, columns), bf16),
            pltpu.VMEM(w_out.shape, bf16),
            pltpu.VMEM((2 * sections, tokens), bf16),
            pltpu.VMEM((parts, chips, sections, block), f32),
            pltpu.VMEM((parts, chips, sections, block), f32),
            pltpu.VMEM((parts, chips - 1, sections, block), bf16),
            pltpu.VMEM((parts, chips - 1, sections, block), bf16),
            pltpu.VMEM((parts, chips, sections, block), f32),
            pltpu.VMEM((sections, width), f32),
            pltpu.VMEM((seq_n, here, width), bf16),
            pltpu.VMEM((seq_n, here, width), bf16),
            pltpu.VMEM((seg_n, here, width), bf16),
            pltpu.VMEM((here, columns + HEAD_DIM), bf16),
            pltpu.VMEM((seq_n, here, columns + HEAD_DIM), bf16),
            pltpu.VMEM((here, columns), bf16),
            pltpu.VMEM((seq_n, here, columns), bf16),
            pltpu.VMEM((sections, kv), f32),
            pltpu.VMEM((seg_n, here, width), bf16),
            dma((IN_FLIGHT,)), dma((2,)),
            dma, dma((parts, chips)), dma, dma((parts,)),
            dma, dma, dma, dma, dma, dma, dma, dma, dma, dma,
        ],
        compiler_params=pltpu.CompilerParams(
            collective_id=0, has_side_effects=True, vmem_limit_bytes=53 * 1024 * 1024
        ),
    )(
        hidden, small, w_in, w_query, w_key, w_value, w_out,
    )


def solution(mesh):
    in_specs = (
        P("segment", "seq", None),
        P(),
        P(),
        P("seq"),
        P("seq", None),
        P(),
        P(None, "segment"),
        P(None, "segment"),
        P(None, "segment"),
        P("segment", None),
    )
    out_specs = P("seq", None)
    return jax.shard_map(shards, mesh=mesh, in_specs=in_specs, out_specs=out_specs, check_vma=False)
```

```python
import functools
import jax
import jax.numpy as jnp
from jax import lax
from jax.experimental import pallas as pl
from jax.experimental.pallas import tpu as pltpu
from jax.sharding import PartitionSpec as P

HEAD_DIM = 128
MESH = pl.DeviceIdType.MESH
IN_FLIGHT = 4
LAG = 1
HALVES = 1
GREET = 0


def chip_order(chip, chips):
    if chips & (chips - 1):
        return [(chip, lax.rem(chip + 1 + k, chips)) for k in range(chips)]
    order = []
    for mask in range(chips - 1, -1, -1):
        other, bit = chip, 1
        while bit < chips:
            if mask & bit:
                other = other + bit * (1 - 2 * lax.rem(lax.div(chip, bit), 2))
            bit *= 2
        order.append(other)
    return order


def kernel(
    seg_n, seq_n, docs, spans, here,
    hidden, small, w_in, w_query, w_key, w_value, w_out,
    out_ref,
    hid, win, wqkv, wout, weights,
    pair_send, pair_recv, line_send, line_recv, kept, product, proj_send, proj_recv, rows_all,
    key_send, key_recv, value_send, value_recv, kv_all, term_recv,
    load_sem, weight_sem, pair_ss, pair_rs, line_ss, line_rs,
    proj_ss, proj_rs, rows_ss, rows_rs, key_ss, key_rs, value_ss, value_rs, term_ss, term_rs,
):
    seg = lax.axis_index("segment")
    q = lax.axis_index("seq")
    core = lax.rem(q, 2)
    chip = lax.div(q, 2)
    chips = seq_n // 2
    partner = q + 1 - 2 * core
    tokens = hidden.shape[1]
    blocks, _, width = hid.shape
    parts = blocks // seq_n
    features = width * parts
    sections = here * seq_n
    f32, bf16 = jnp.float32, jnp.bfloat16

    seg_order = chip_order(seg, seg_n)[: seg_n - 1]

    def seg_peer(d):
        return seg_order[d - 1]

    def seq_peer(d):
        return lax.rem(q + d, seq_n)

    others = chip_order(chip, chips)

    units = [(p, k) for p in range(parts) for k in range(chips - 1)] + [(p, chips - 1) for p in range(parts)]
    order = [("peer", units[0])]
    for i in range(1, len(units)):
        order += [("peer", units[i]), ("own", units[i - 1])]
    order.append(("own", units[-1]))

    def load(i):
        kind, (p, k) = order[i]
        block = (others[k] * 2 + (core if kind == "own" else 1 - core)) * parts + p
        return pltpu.make_async_copy(
            hidden.at[0, :, pl.ds(pl.multiple_of(block * width, 128), width)],
            hid.at[i],
            load_sem.at[i % IN_FLIGHT],
        )

    weight_loads = [
        pltpu.make_async_copy(source, target, weight_sem.at[min(i, 1)])
        for i, (source, target) in enumerate((
            (w_in, win), (w_key, wqkv.at[1]), (w_value, wqkv.at[2]), (w_query, wqkv.at[0]),
            (w_out, wout)))
    ]
    for i in range(min(IN_FLIGHT, blocks)):
        load(i).start()

    barrier = pltpu.get_barrier_semaphore()
    for d in range(1, seg_n):
        pl.semaphore_signal(barrier, inc=1, device_id=(seg_peer(d), q), device_id_type=MESH)
    for d in range(1, seq_n):
        pl.semaphore_signal(barrier, inc=1, device_id=(seg, seq_peer(d)), device_id_type=MESH)

    len_row = small[pl.ds(seg, 1), 0:spans]
    sec_row = small[pl.ds(docs + seg, 1), 0:spans]
    c_row = lax.broadcasted_iota(jnp.int32, (spans, spans), 0)
    c_col = lax.broadcasted_iota(jnp.int32, (spans, spans), 1)
    len_all = jnp.broadcast_to(len_row, (spans, spans))
    ends = jnp.sum(jnp.where(c_col <= c_row, len_all, 0.0), axis=1, keepdims=True)
    starts = jnp.sum(jnp.where(c_col < c_row, len_all, 0.0), axis=1, keepdims=True)
    position = (q * tokens + lax.broadcasted_iota(jnp.int32, (spans, tokens), 1)).astype(f32)
    member = jnp.where((position >= starts) & (position < ends), 1.0, 0.0).astype(bf16)
    s_row = lax.broadcasted_iota(jnp.int32, (sections, spans), 0).astype(f32)
    count = jnp.zeros((sections, 1), f32)
    for d in range(docs):
        same = s_row == small[docs + d : docs + d + 1, 0:spans]
        count += jnp.sum(jnp.where(same, 1.0, 0.0), axis=1, keepdims=True)
    share = jnp.where(s_row == sec_row, 1.0 / (len_row * jnp.maximum(count, 1.0)), 0.0)
    high = share.astype(bf16)
    low = (share - high.astype(f32)).astype(bf16)
    weights[...] = jnp.dot(
        jnp.concatenate([high, low], axis=0), member, preferred_element_type=f32
    ).astype(bf16)

    def pair_copy(p, k):
        return pltpu.make_async_remote_copy(
            pair_send.at[p, k], pair_recv.at[p, k], pair_ss, pair_rs.at[p, k],
            device_id=(seg, partner), device_id_type=MESH)

    def line_copy(p, k):
        return pltpu.make_async_remote_copy(
            line_send.at[p, k], line_recv.at[p, k], line_ss, line_rs.at[p],
            device_id=(seg, others[k] * 2 + core), device_id_type=MESH)

    def drain(ref, sem):
        pltpu.make_async_copy(ref, ref, sem).wait()

    def finish(p, k):
        pair_copy(p, k).wait_recv()
        part = kept[p, k] + pair_recv[p, k].astype(f32)
        if k < chips - 1:
            line_send[p, k] = part.astype(bf16)
            line_copy(p, k).start()
        else:
            kept[p, k] = part

    ended = []
    for i, (kind, (p, k)) in enumerate(order):
        load(i).wait()
        if i + IN_FLIGHT < blocks:
            load(i + IN_FLIGHT).start()
        if i == blocks - 3:
            weight_loads[0].start()
        both = jnp.dot(weights[...], hid[i], preferred_element_type=f32)
        part = both[:sections] + both[sections:]
        if kind == "own":
            kept[p, k] = part
            if k < chips - 1:
                finish(p, k)
            continue
        pair_send[p, k] = part.astype(bf16)
        if i == 0:
            pl.semaphore_wait(barrier, seg_n + seq_n - 2)
        pair_copy(p, k).start()
    for p in range(parts):
        finish(p, chips - 1)
    ended += [(pair_send, pair_ss), (line_send, line_ss)]
    weight_loads[0].wait()
    for w in weight_loads[1:]:
        w.start()
    depth = product.shape[1]
    half = depth // HALVES

    def proj_copy(d, n):
        cut = pl.ds(n * half, half)
        return pltpu.make_async_remote_copy(
            proj_send.at[seq_peer(d), :, cut], proj_recv.at[q, :, cut], proj_ss, proj_rs,
            device_id=(seg, seq_peer(d)), device_id_type=MESH)

    far_first = []
    for k in range(chips - 1):
        for c in range(2):
            far_first.append(lax.rem(others[k] * 2 + c - q + seq_n, seq_n))
    far_first.append(lax.rem(partner - q + seq_n, seq_n))
    rest = pl.ds(0, seq_n - 1)
    for p in range(parts):
        drain(line_recv.at[p], line_rs.at[p])
        total = kept[p, chips - 1]
        for k in range(chips - 1):
            total += line_recv[p, k].astype(f32)
        total = total.astype(bf16)
        for n in range(HALVES):
            cut = slice(n * half, (n + 1) * half)
            term = jnp.dot(total, win[p * width : (p + 1) * width, cut], preferred_element_type=f32)
            if p:
                term = term + product[:, cut]
            if p < parts - 1:
                product[:, cut] = term
                continue
            for s in range(seq_n):
                proj_send[s, :, cut] = term[s * here : (s + 1) * here, :].astype(bf16)
            for d in far_first:
                proj_copy(d, n).start()
    proj_recv[q] = proj_send[q]
    ended.append((proj_send.at[rest], proj_ss))
    drain(proj_recv.at[rest], proj_rs)
    partial = proj_recv[0].astype(f32)
    for s in range(1, seq_n):
        partial += proj_recv[s].astype(f32)
    rows_all[seg] = partial.astype(bf16)

    def rows_copy(d):
        return pltpu.make_async_remote_copy(
            rows_all.at[seg], rows_all.at[seg], rows_ss, rows_rs,
            device_id=(seg_peer(d), q), device_id_type=MESH)

    for d in range(1, seg_n):
        rows_copy(d).start()
    ended.append((rows_all.at[pl.ds(0, seg_n - 1)], rows_ss))
    drain(rows_all.at[pl.ds(0, seg_n - 1)], rows_rs)
    section_in = rows_all[0].astype(f32)
    for s in range(1, seg_n):
        section_in += rows_all[s].astype(f32)
    lanes = small.shape[1]
    first, rows = 2 * docs + 8, section_in.shape[1] // lanes
    scale = lax.rsqrt(jnp.mean(section_in * section_in, axis=1, keepdims=True) + 1e-05)
    normed = (section_in * jnp.concatenate([small[i : i + 1, 0:lanes] for i in range(first, first + rows)], axis=1)).astype(bf16)
    columns = wqkv.shape[2]
    heads = columns // HEAD_DIM
    live_row = jnp.broadcast_to(small[2 * docs : 2 * docs + 1, 0:HEAD_DIM], (here, HEAD_DIM))
    on_diagonal = lax.broadcasted_iota(jnp.int32, (here, HEAD_DIM), 0) == lax.broadcasted_iota(
        jnp.int32, (here, HEAD_DIM), 1)
    live = jnp.sum(jnp.where(on_diagonal, live_row, 0.0), axis=1, keepdims=True)

    def spread_copy(source, target, send, receive, d):
        return pltpu.make_async_remote_copy(
            source, target.at[q], send, receive,
            device_id=(seg, seq_peer(d)), device_id_type=MESH)

    drain(wqkv, weight_sem.at[1])
    drain(wout, weight_sem.at[1])
    key_send[:, 0:columns] = (scale * jnp.dot(normed, wqkv[1], preferred_element_type=f32)).astype(bf16)
    key_send[:, columns:] = jnp.broadcast_to(live, (here, HEAD_DIM)).astype(bf16)
    for d in far_first:
        spread_copy(key_send, key_recv, key_ss, key_rs, d).start()
    value_send[...] = (scale * jnp.dot(normed, wqkv[2], preferred_element_type=f32)).astype(bf16)
    for d in far_first:
        spread_copy(value_send, value_recv, value_ss, value_rs, d).start()
    key_recv[q] = key_send[...]
    value_recv[q] = value_send[...]
    ended += [(key_recv.at[rest], key_ss), (value_recv.at[rest], value_ss)]
    stacked = heads * here
    own_head = lax.div(lax.broadcasted_iota(jnp.int32, (stacked, columns), 0), here) == lax.div(
        lax.broadcasted_iota(jnp.int32, (stacked, columns), 1), HEAD_DIM)
    queries = scale * jnp.dot(normed, wqkv[0], preferred_element_type=f32)
    queries = jnp.where(own_head, jnp.concatenate([queries] * heads, axis=0), 0.0).astype(bf16)
    own = q * here + lax.rem(lax.broadcasted_iota(jnp.int32, (stacked, sections), 0), here)
    drain(key_recv.at[rest], key_rs)
    for s in range(seq_n):
        kv_all[s * here : (s + 1) * here, 0 : columns + HEAD_DIM] = key_recv[s].astype(f32)
    across = (((1,), (1,)), ((), ()))
    live_sum = lax.dot_general(
        jnp.ones((stacked, HEAD_DIM), bf16), kv_all[:, columns : columns + HEAD_DIM].astype(bf16), across,
        preferred_element_type=f32)
    allowed = (live_sum > 0) | (lax.broadcasted_iota(jnp.int32, (stacked, sections), 1) == own)
    scores = lax.dot_general(
        queries, kv_all[:, 0:columns].astype(bf16), across, preferred_element_type=f32)
    scores = jnp.where(allowed, scores / jnp.sqrt(f32(HEAD_DIM)), f32(-1e30))
    grown = jnp.exp(scores - jnp.max(scores, axis=1, keepdims=True))
    probs = (grown / jnp.sum(grown, axis=1, keepdims=True)).astype(bf16)
    drain(value_recv.at[rest], value_rs)
    for s in range(seq_n):
        kv_all[s * here : (s + 1) * here, columns + HEAD_DIM :] = value_recv[s].astype(f32)
    mixed = jnp.dot(probs, kv_all[:, columns + HEAD_DIM :].astype(bf16), preferred_element_type=f32)
    mixed = jnp.where(own_head, mixed, 0.0)
    attended = mixed[0:here]
    for h in range(1, heads):
        attended += mixed[h * here : (h + 1) * here]
    terms = jnp.dot(attended.astype(bf16), wout[...], preferred_element_type=f32)
    term_recv[seg] = terms.astype(bf16)

    def term_copy(d):
        return pltpu.make_async_remote_copy(
            term_recv.at[seg], term_recv.at[seg], term_ss, term_rs,
            device_id=(seg_peer(d), q), device_id_type=MESH)

    for d in range(1, seg_n):
        term_copy(d).start()
    ended.append((term_recv.at[pl.ds(0, seg_n - 1)], term_ss))
    drain(term_recv.at[pl.ds(0, seg_n - 1)], term_rs)
    combined = term_recv[0].astype(f32)
    for s in range(1, seg_n):
        combined += term_recv[s].astype(f32)
    out_ref[...] = (section_in + combined).astype(out_ref.dtype)

    for ref, sem in ended:
        drain(ref, sem)


def shards(
    hidden, span_lengths, section_of, section_live, w_in, norm_gain, w_query, w_key, w_value, w_out
):
    seg_n, seq_n = lax.axis_size("segment"), lax.axis_size("seq")
    tokens, depth = hidden.shape[1:]
    docs, spans = span_lengths.shape
    lanes = max(128, spans)

    gains = norm_gain.reshape(-1, lanes)
    total_rows = 2 * docs + 8 + gains.shape[0]

    def padded(entries, row):
        return jnp.pad(
            entries, ((row, total_rows - row - entries.shape[0]), (0, lanes - entries.shape[1])))

    whole = (padded(span_lengths, 0) + padded(section_of, docs)) + padded(section_live.reshape(1, -1), 2 * docs)
    small = whole.astype(jnp.float32) + padded(gains, 2 * docs + 8)
    here = section_live.shape[0]
    sections = here * seq_n
    chips = seq_n // 2
    features = depth // seq_n
    parts = max(features // 512, 1)
    block = features // parts
    width, columns = w_query.shape
    bf16, f32 = jnp.bfloat16, jnp.float32
    vmem = pl.BlockSpec(memory_space=pltpu.VMEM)
    hbm = pl.BlockSpec(memory_space=pl.ANY)
    dma = pltpu.SemaphoreType.DMA
    kv = 2 * columns + HEAD_DIM
    return pl.pallas_call(
        functools.partial(kernel, seg_n, seq_n, docs, spans, here),
        out_shape=jax.ShapeDtypeStruct((here, width), bf16),
        in_specs=[hbm, vmem] + [hbm] * 5,
        out_specs=vmem,
        scratch_shapes=[
            pltpu.VMEM((seq_n * parts, tokens, block), bf16),
            pltpu.VMEM(w_in.shape, bf16),
            pltpu.VMEM((3, width, columns), bf16),
            pltpu.VMEM(w_out.shape, bf16),
            pltpu.VMEM((2 * sections, tokens), bf16),
            pltpu.VMEM((parts, chips, sections, block), bf16),
            pltpu.VMEM((parts, chips, sections, block), bf16),
            pltpu.VMEM((parts, chips - 1, sections, block), bf16),
            pltpu.VMEM((parts, chips - 1, sections, block), bf16),
            pltpu.VMEM((parts, chips, sections, block), f32),
            pltpu.VMEM((sections, width), f32),
            pltpu.VMEM((seq_n, here, width), bf16),
            pltpu.VMEM((seq_n, here, width), bf16),
            pltpu.VMEM((seg_n, here, width), bf16),
            pltpu.VMEM((here, columns + HEAD_DIM), bf16),
            pltpu.VMEM((seq_n, here, columns + HEAD_DIM), bf16),
            pltpu.VMEM((here, columns), bf16),
            pltpu.VMEM((seq_n, here, columns), bf16),
            pltpu.VMEM((sections, kv), f32),
            pltpu.VMEM((seg_n, here, width), bf16),
            dma((IN_FLIGHT,)), dma((2,)),
            dma, dma((parts, chips)), dma, dma((parts,)),
            dma, dma, dma, dma, dma, dma, dma, dma, dma, dma,
        ],
        compiler_params=pltpu.CompilerParams(
            collective_id=0, has_side_effects=True, vmem_limit_bytes=53 * 1024 * 1024
        ),
    )(
        hidden, small, w_in, w_query, w_key, w_value, w_out,
    )


def solution(mesh):
    in_specs = (
        P("segment", "seq", None),
        P(),
        P(),
        P("seq"),
        P("seq", None),
        P(),
        P(None, "segment"),
        P(None, "segment"),
        P(None, "segment"),
        P("segment", None),
    )
    out_specs = P("seq", None)
    return jax.shard_map(shards, mesh=mesh, in_specs=in_specs, out_specs=out_specs, check_vma=False)
```
